768 devices in a mesh: gx: 8 (over x, core), gy: 12 (over z), gz: 8 (over y).
Axes of the slice: x: 4, y: 8, z: 12, core: 2. Of those that a mesh axis runs over, the one named last changes fastest.
Arguments:
- fine_blocks: float32 [16, 24, 32, 7, 4096], P('gx', 'gy', 'gz'), may hold values from -0.75 to 0.75
- prolong: float32 [16, 24, 32, 1024], P('gx', 'gy', 'gz'), may hold values from -1.5 to 1.5
- agg_map: int32 [16, 24, 32], replicated, may hold values from 0 to 7, as said below
- owner_map: int32 [8, 12, 64], P('gx', 'gy', 'gz'), may hold values from 0 to 7, as said below
Outputs:
- coarse_rows: float32 [8, 12, 64, 14336], P('gx', 'gy', 'gz')
The draws below stay inside these ranges and needn't reach their ends.
Inputs may be any that keep to these rules, and one draw needn't show every extreme that they name: `agg_map`: every one of the 8 slots of each brick names at least one element of that brick. `owner_map`: owners are devices with the same gx and gy indices as the brick. Each brick gives exactly 1 of its slots to each owner. The elements of one brick whose rows go to one owner number at most 4, and exactly 4 for one owner of every brick.
All inputs are finite; a program needn't handle non-finite values.
Results may differ from the reference program's by a relative error of at most 0.0001.
Values sent between devices are 32-bit elements; how exact they have to be, the bound alone decides.
A program may use at most 32 MiB of HBM per device.

```python
import jax
import jax.numpy as jnp
from jax import lax

DOF = 64
CDOF = 16
BX = 2
BY = 2
BZ = 4
AGGS = 8
NX = 16
NY = 24
NZ = 32


def layout_plan(key):
    bricks_x = NX // BX
    bricks_y = NY // BY
    bricks_z = NZ // BZ
    group_size = bricks_z
    elements = BX * BY * BZ
    rows_each = AGGS // group_size
    capacity = min(2 * elements // group_size, elements - (group_size - 1) * rows_each)
    extras = elements - capacity - (group_size - 1) * rows_each
    others_count = group_size - 1
    brick_count = bricks_x * bricks_y * bricks_z

    def one_brick(brick):
        brick_key = jax.random.fold_in(jax.random.fold_in(key, 11), brick)
        keys = jax.random.split(brick_key, 5)
        heavy = jax.random.randint(keys[0], (), 0, group_size)
        offset = jax.random.randint(keys[1], (), 0, others_count)
        others = jnp.arange(others_count, dtype=jnp.int32)
        added = extras // others_count + ((others - offset) % others_count < extras % others_count).astype(jnp.int32)
        targets = (heavy + 1 + others) % group_size
        counts = jnp.full((group_size,), rows_each, jnp.int32).at[targets].add(added).at[heavy].set(capacity)
        labels = jnp.repeat(jnp.arange(group_size, dtype=jnp.int32), counts, total_repeat_length=elements)
        starts = jnp.cumsum(counts) - counts
        ranks = jnp.arange(elements, dtype=jnp.int32) - starts[labels]
        extra_sub = jax.random.randint(keys[2], (elements,), 0, rows_each)
        subslot = jnp.where(ranks < rows_each, ranks, extra_sub)
        slot_perm = jax.random.permutation(keys[3], AGGS).astype(jnp.int32)
        agg_ids = slot_perm[labels * rows_each + subslot]
        element_perm = jax.random.permutation(keys[4], elements)
        placed = agg_ids[element_perm]
        inverse = jnp.argsort(slot_perm).astype(jnp.int32)
        owner_ids = inverse // rows_each
        return (placed.reshape(BX, BY, BZ), owner_ids)
    placed_all, owners_all = jax.vmap(one_brick)(jnp.arange(brick_count, dtype=jnp.int32))
    agg_full = placed_all.reshape(bricks_x, bricks_y, bricks_z, BX, BY, BZ).transpose(0, 3, 1, 4, 2, 5).reshape(NX, NY, NZ)
    owner_full = owners_all.reshape(bricks_x, bricks_y, bricks_z * AGGS)
    return (agg_full.astype(jnp.int32), owner_full.astype(jnp.int32))


def draw_agg_map(key, part):
    return layout_plan(key)[0]


def draw_owner_map(key, part):
    return layout_plan(key)[1]


def block_levels(stream_key, extent, pieces, least, high):
    def one(axis_at, blocks):
        draws = jax.random.uniform(jax.random.fold_in(jax.random.fold_in(stream_key, 6), axis_at), (blocks,), jnp.float32, least / len(pieces), high / len(pieces))
        return jnp.repeat(jnp.exp(draws), extent[axis_at] // blocks).reshape((-1,) + (1,) * (len(extent) - axis_at - 1))

    loudness = one(*pieces[0])
    for cut in pieces[1:]:
        loudness = loudness * one(*cut)
    return loudness


def gaussian(key, dims, width, bound, cuts=(), kind=jnp.bfloat16):
    values = width * jax.random.normal(key, dims, jnp.float32)
    if cuts:
        values = values * block_levels(key, dims, cuts, -0.22, 0.18)
    return jnp.clip(values, -bound, bound).astype(kind)


def setup_inputs(seed: int = 0) -> dict:
    arg_keys = jax.random.split(jax.random.key(seed), 5)
    return {
        "fine_blocks": gaussian(arg_keys[0], (NX, NY, NZ, 7, DOF * DOF), DOF ** -0.5, 0.75, ((0, 8), (1, 12), (2, 8)), jnp.float32),
        "prolong": gaussian(arg_keys[1], (NX, NY, NZ, DOF * CDOF), 0.25, 1.5, ((0, 8), (1, 12), (2, 8)), jnp.float32),
        "agg_map": draw_agg_map(jax.random.fold_in(arg_keys[4], 71), 0),
        "owner_map": draw_owner_map(jax.random.fold_in(arg_keys[4], 71), 0),
    }


face_steps = ((0, 0, 0), (-1, 0, 0), (1, 0, 0), (0, -1, 0), (0, 1, 0), (0, 0, -1), (0, 0, 1))


def reference(fine_blocks, prolong, agg_map, owner_map):
    bricks_x = NX // BX
    bricks_y = NY // BY
    bricks_z = NZ // BZ
    rows_each = AGGS // bricks_z
    blocks = fine_blocks.reshape(NX, NY, NZ, 7, DOF, DOF)
    bases = prolong.reshape(NX, NY, NZ, DOF, CDOF)
    padded = jnp.pad(bases, ((1, 1), (1, 1), (1, 1), (0, 0), (0, 0)))

    def plane(index):
        block_plane = lax.dynamic_index_in_dim(blocks, index, 0, keepdims=False)
        window = lax.dynamic_slice_in_dim(padded, index, 3, 0)
        beside = jnp.stack([window[1 + sx, 1 + sy:1 + sy + NY, 1 + sz:1 + sz + NZ] for sx, sy, sz in face_steps], axis=2)
        products = jnp.einsum('yzkij,yzkjc->yzkic', block_plane, beside, precision=lax.Precision.HIGHEST)
        own_base = window[1, 1:NY + 1, 1:NZ + 1]
        coarse = jnp.einsum('yzic,yzkid->yzkcd', own_base, products, precision=lax.Precision.HIGHEST)
        return coarse.reshape(NY, NZ, 7, CDOF * CDOF)

    terms = lax.map(plane, jnp.arange(NX, dtype=jnp.int32))
    padded_agg = jnp.pad(agg_map, 1)
    coord_x = jnp.arange(NX, dtype=jnp.int32)[:, None, None]
    coord_y = jnp.arange(NY, dtype=jnp.int32)[None, :, None]
    coord_z = jnp.arange(NZ, dtype=jnp.int32)[None, None, :]
    columns = []
    for face, (sx, sy, sz) in enumerate(face_steps):
        neighbour = padded_agg[1 + sx:1 + sx + NX, 1 + sy:1 + sy + NY, 1 + sz:1 + sz + NZ]
        inside = ((coord_x % BX + sx >= 0) & (coord_x % BX + sx < BX) & (coord_y % BY + sy >= 0) & (coord_y % BY + sy < BY) & (coord_z % BZ + sz >= 0) & (coord_z % BZ + sz < BZ))
        relation = jnp.where(inside, 0, face).astype(jnp.int32)
        columns.append(relation * AGGS + neighbour)
    column_slot = jnp.stack(columns, axis=3).astype(jnp.int32)
    owners = owner_map.reshape(bricks_x, bricks_y, bricks_z, AGGS)
    slot_ids = jnp.arange(AGGS, dtype=jnp.int32)
    earlier = (owners[..., None, :] == owners[..., :, None]) & (slot_ids[None, :] < slot_ids[:, None])
    rank_in_owner = jnp.sum(earlier.astype(jnp.int32), axis=-1)
    brick_x = jnp.broadcast_to(coord_x // BX, (NX, NY, NZ))
    brick_y = jnp.broadcast_to(coord_y // BY, (NX, NY, NZ))
    brick_z = jnp.broadcast_to(coord_z // BZ, (NX, NY, NZ))
    owner_of = owners[brick_x, brick_y, brick_z, agg_map]
    rank_of = rank_in_owner[brick_x, brick_y, brick_z, agg_map]
    row_slot = ((brick_x * bricks_y + brick_y) * bricks_z + owner_of) * AGGS + brick_z * rows_each + rank_of
    row_slot = row_slot.astype(jnp.int32)
    total_rows = bricks_x * bricks_y * bricks_z * AGGS
    result = jnp.zeros((total_rows, 7 * AGGS, CDOF * CDOF), jnp.float32)
    row_index = jnp.broadcast_to(row_slot[..., None], column_slot.shape)
    result = result.at[row_index, column_slot].add(terms)
    return result.reshape(bricks_x, bricks_y, bricks_z * AGGS, 7 * AGGS * CDOF * CDOF)
```

```python
import functools

import jax
import jax.numpy as jnp
from jax import lax
from jax.experimental import pallas as pl
from jax.experimental.pallas import tpu as pltpu
from jax.sharding import PartitionSpec as P

MESH = pl.DeviceIdType.MESH
F32 = jnp.float32
BF16 = jnp.bfloat16
AGGS = 8
FACES = 7
STEPS = ((0, 0, 0), (-1, 0, 0), (1, 0, 0), (0, -1, 0), (0, 1, 0), (0, 0, -1), (0, 0, 1))
ORDER = (4, 3, 5, 2, 6, 1, 7)
INNER = tuple((x, k) for x in range(2) for k in range(FACES) if (x, k) not in ((0, 1), (1, 2)))


def iota(shape, dim):
    return lax.broadcasted_iota(jnp.int32, shape, dim)


def split(value):
    high = value.astype(BF16)
    return high, (value - high.astype(F32)).astype(BF16)


def dot(a, b):
    return jnp.dot(a, b, preferred_element_type=F32)


def columns_of(slab):
    row, group = iota((64, 128), 0) & 7, iota((64, 128), 1) >> 4
    for bit in (4, 2, 1):
        row_bit, group_bit = row & bit, group & bit
        down = pltpu.roll(pltpu.roll(slab, 128 - 16 * bit, 1), bit, 0)
        up = pltpu.roll(pltpu.roll(slab, 16 * bit, 1), 64 - bit, 0)
        slab = jnp.where(row_bit == group_bit, slab, jnp.where(row_bit > 0, down, up))
    return slab


def stacked(cols):
    high, low = split(cols)
    return jnp.concatenate([high, low, high, low], axis=0)


def kernel(
    sizes, a_hbm, p_hbm, agg_hbm, own_hbm, out_ref,
    a_v, slabs, agg_v, own_v, acat, ycat, tcat, scat, msg, recv,
    local_sem, halo_send, halo_recv, send_sem, recv_sem, ready,
):
    nx, ny, nz = sizes
    gx, gy, gz = lax.axis_index("gx"), lax.axis_index("gy"), lax.axis_index("gz")

    def device(dx, dy, dz):
        return (
            lax.rem(gx + dx + nx, nx),
            lax.rem(gy + dy + ny, ny),
            lax.rem(gz + dz + nz, nz),
        )

    def signal(sem, target):
        pl.semaphore_signal(sem, inc=1, device_id=target, device_id_type=MESH)

    barrier = pltpu.get_barrier_semaphore()
    for step in STEPS[1:]:
        signal(barrier, device(*step))

    prolong_copies, fine_copies, index_copies = [], [], []
    for x in range(2):
        for y in range(2):
            c = x * 2 + y
            prolong_copies.append(
                pltpu.make_async_copy(
                    p_hbm.at[x, y], slabs.at[x, :, pl.ds(4 * y, 4), :], local_sem.at[c]
                )
            )
            rows = pl.ds(c * 896, 896)
            fine_copies.append(
                pltpu.make_async_copy(a_hbm.at[rows], a_v.at[rows], local_sem.at[4 + c])
            )
    for plane in range(4):
        where = jnp.clip(gx * 2 - 1 + plane, 0, 2 * nx - 1)
        index_copies.append(
            pltpu.make_async_copy(
                agg_hbm.at[pl.ds(where, 1)], agg_v.at[pl.ds(plane, 1)], local_sem.at[8 + plane]
            )
        )
    index_copies.append(pltpu.make_async_copy(own_hbm, own_v, local_sem.at[12]))
    for copy in prolong_copies + fine_copies + index_copies:
        copy.start()

    pl.semaphore_wait(barrier, 6)

    halo = []

    def halo_copy(src, dst, target):
        n = len(halo)
        halo.append(
            pltpu.make_async_remote_copy(
                src_ref=src, dst_ref=dst, send_sem=halo_send.at[n], recv_sem=halo_recv.at[n],
                device_id=target, device_id_type=MESH,
            )
        )
        halo[-1].start()

    for u in range(2):
        half = pl.ds(4 * u, 4)
        halo_copy(p_hbm.at[u, 1], slabs.at[4, :, half, :], device(0, 1, 0))
        halo_copy(p_hbm.at[u, 0], slabs.at[5, :, half, :], device(0, -1, 0))
        halo_copy(p_hbm.at[1, u], slabs.at[2, :, half, :], device(1, 0, 0))
        halo_copy(p_hbm.at[0, u], slabs.at[3, :, half, :], device(-1, 0, 0))
        for v in range(2):
            halo_copy(p_hbm.at[u, v, :, 3, :], slabs.at[6, :, u * 2 + v, :], device(0, 0, 1))
            halo_copy(p_hbm.at[u, v, :, 0, :], slabs.at[6, :, 4 + u * 2 + v, :], device(0, 0, -1))

    def greet(stage):
        for step in (-1, 1):
            signal(ready.at[stage], device(0, 0, step))

    greet(0)

    for copy in prolong_copies:
        copy.wait()
    own_cols = [columns_of(slabs[x].reshape(64, 128)) for x in range(2)]
    own_rhs = [stacked(cols) for cols in own_cols]
    turned = jnp.concatenate(split(jnp.concatenate(own_cols, axis=0).T), axis=0)
    lane = iota((128, 256), 1)
    spot = 2 * ((lane & 127) >> 2) + (lane >> 7)
    keep = ((iota((256, 256), 0) >> 4) & 3) == (iota((256, 256), 1) & 3)
    left = {}
    for x in range(2):
        spread = (iota((128, 256), 0) == spot + 64 * x).astype(BF16)
        wide = jnp.where(keep, dot(turned, spread), 0.0).astype(BF16)
        for y in range(2):
            parts = []
            for at in (y * 64, 128 + y * 64):
                rows = wide[at : at + 64]
                parts.append(jnp.concatenate([rows[:, :128], rows[:, 128:]], axis=0))
            left[x, y] = parts

    pl.semaphore_wait(ready.at[0], 2)
    greet(1)

    low_lanes = iota((64, 128), 1) < 64
    for x in range(2):
        for y in range(2):
            c = x * 2 + y
            fine_copies[c].wait()
            for k in range(FACES):
                high, low = split(a_v[pl.ds((c * FACES + k) * 128, 128), :])
                acat[c, 0:128, k * 128 : (k + 1) * 128] = high
                acat[c, 128:256, k * 128 : (k + 1) * 128] = low
            high, low = left[x, y]
            both = dot(jnp.concatenate([high, high], axis=1), acat[c]) + dot(low, acat[c, 0:128])
            for k in range(FACES):
                tile = both[:, k * 128 : (k + 1) * 128]
                tile = jnp.where(low_lanes, tile[0:64], tile[64:128])
                tile = tile + pltpu.roll(tile, 64, 1)
                high, low = split(tile)
                ycat[k, x, y * 64 : y * 64 + 64, 0:128] = high
                ycat[k, x, y * 64 : y * 64 + 64, 128:256] = low

    pl.semaphore_wait(ready.at[1], 2)
    greet(2)

    for copy in index_copies:
        copy.wait()
    agg_rows = agg_v[...].reshape(4 * 2 * ny, 4 * nz).astype(F32).astype(BF16)
    shape = (16, 4 * 2 * ny)
    line = iota(shape, 0)
    take = iota(shape, 1) == (line >> 2) * (2 * ny) + gy * 2 - 1 + (line & 3)
    near = dot(take.astype(BF16), agg_rows).astype(BF16)
    shape = (4 * nz, 384)
    lane = iota(shape, 1)
    take = iota(shape, 0) == gz * 4 + ((lane >> 3) & 3) + (lane >> 7) - 1
    near = dot(near, take.astype(BF16))
    lane = iota((1, 128), 1)
    element, z_at, y_high = (lane >> 3) & 7, (lane >> 3) & 3, ((lane >> 5) & 1) == 1

    def slot(x, dx, dy, dz):
        lanes = slice((dz + 1) * 128, (dz + 2) * 128)
        row = (x + 1 + dx) * 4 + 1 + dy
        return jnp.where(y_high, near[row + 1 : row + 2, lanes], near[row : row + 1, lanes])

    slots = [[slot(x, *step) for step in STEPS] for x in range(2)]
    owners = own_v[0].astype(F32)
    owner = [jnp.zeros((1, 128), F32)] * 2
    for s in range(AGGS):
        value = jnp.broadcast_to(owners[:, s : s + 1], (1, 128))
        owner = [jnp.where(slots[x][0] == s, value, owner[x]) for x in range(2)]
    place = [jnp.zeros((1, 128), F32)] * 2
    for m in range(AGGS):
        turn = [pltpu.roll(owner[x], 8 * m, 1) if m else owner[x] for x in range(2)]
        if m:
            for x in range(2):
                place[x] += jnp.where((turn[x] == owner[x]) & (element >= m), 1.0, 0.0)
        place[1] += jnp.where(turn[0] == owner[1], 1.0, 0.0)
    code = [owner[x] * 8.0 + place[x] for x in range(2)]

    row64 = iota((64, 128), 0).astype(F32)

    def selection(codes):
        return (row64 == codes).astype(BF16)

    for n, (x, k) in enumerate(INNER):
        codes = owner[x] * 8.0 + slots[x][k]
        valid = {3: y_high, 4: ~y_high, 5: z_at >= 1, 6: z_at <= 2}.get(k)
        if valid is not None:
            codes = jnp.where(valid, codes, -1.0)
        scat[:, n * 128 : (n + 1) * 128] = selection(codes)

    fold = ((iota((256, 128), 0) & 15) == (iota((256, 128), 1) & 15)).astype(BF16)
    row_e, lane_e = iota((128, 128), 0) >> 4, iota((128, 128), 1) >> 4
    on_c = (iota((128, 128), 0) & 7) == lane_e

    def terms(lhs, rhs, shift):
        block = jnp.where(row_e + shift == lane_e, dot(lhs, rhs), 0.0)
        tall = jnp.where(on_c, dot(jnp.concatenate(split(block), axis=1), fold), 0.0)
        tall = tall.reshape(8, 16, 128)
        tall = jnp.concatenate(
            [tall[:, 0:8].reshape(64, 128), tall[:, 8:16].reshape(64, 128)], axis=1
        )
        return jnp.concatenate(split(tall), axis=0)

    shifts = {3: -4, 4: 4, 5: -1, 6: 1}
    for n, (x, k) in enumerate(INNER):
        other = {1: 0, 2: 1}.get(k, x)
        tcat[n * 128 : (n + 1) * 128, :] = terms(ycat[k, x], own_rhs[other], shifts.get(k, 0))

    copies = []

    def send(stage, rows):
        for o in range(AGGS):
            for h in range(2):
                msg[pl.ds(o * 48 + stage * 16 + h * 8, 8), :] = rows[
                    o * 8 : o * 8 + 8, h * 128 : (h + 1) * 128
                ]
        target_rows = pl.ds(pl.multiple_of(gz * 48 + stage * 16, 16), 16)
        for d in ORDER:
            target = device(0, 0, d)
            copy = pltpu.make_async_remote_copy(
                src_ref=msg.at[pl.ds(pl.multiple_of(target[2] * 48 + stage * 16, 16), 16)],
                dst_ref=recv.at[target_rows],
                send_sem=send_sem.at[stage, d], recv_sem=recv_sem.at[stage, d],
                device_id=target, device_id_type=MESH,
            )
            copy.start()
            copies.append(copy)
        copy = pltpu.make_async_copy(
            msg.at[target_rows], recv.at[target_rows], recv_sem.at[stage, 0]
        )
        copy.start()
        copies.append(copy)

    pl.semaphore_wait(ready.at[2], 2)
    send(0, dot(scat[...], tcat[...]))

    inside = (gx > 0, gx < nx - 1, gy > 0, gy < ny - 1, gz > 0, gz < nz - 1)

    def when(flag, value, other):
        return jnp.where(jnp.full((1, 128), flag), value, other)

    label = [
        [
            when(inside[0], slots[0][1] + 1.0, 0.0),
            when(inside[1], slots[1][2] + 9.0, 0.0),
        ],
        [
            jnp.where(
                y_high,
                when(inside[3], slots[x][4] + 9.0, 0.0),
                when(inside[2], slots[x][3] + 1.0, 0.0),
            )
            for x in range(2)
        ],
        [
            jnp.where(
                z_at == 0,
                when(inside[4], slots[x][5] + 1.0, 0.0),
                jnp.where(z_at == 3, when(inside[5], slots[x][6] + 9.0, 0.0), 0.0),
            )
            for x in range(2)
        ],
    ]
    row, lane_all = iota((128, 128), 0), iota((128, 128), 1)
    once = ((lane_all & 7) == 0) & (lane_all < 64)
    which, who = [], []
    for x in range(2):
        value = jnp.where(
            row < 4, label[0][x], jnp.where(row < 8, label[1][x], jnp.where(row < 12, label[2][x], 0.0))
        )
        value = jnp.where(once & ((row & 3).astype(F32) == place[x]), value, 0.0)
        which.append(value.astype(BF16))
        row_o = iota((64, 128), 0)
        who.append((((row_o & 7) == 4) & ((row_o >> 3).astype(F32) == owner[x])).astype(BF16))
    labels = lax.dot_general(
        jnp.concatenate(who, axis=1), jnp.concatenate(which, axis=1),
        (((1,), (1,)), ((), ())), preferred_element_type=F32,
    )

    edge_codes = [
        code[0],
        code[1],
        jnp.where(y_high, pltpu.roll(code[1], 32, 1), code[0]) + 4.0,
        jnp.where(y_high, code[1], pltpu.roll(code[0], 96, 1)) + 4.0,
    ]
    edge_codes = [when(inside[i], edge_codes[i], -1.0) for i in range(4)]
    z_code = jnp.full((1, 128), -1.0, F32)
    for side in range(2):
        for x in range(2):
            for y in range(2):
                to, at = side * 4 + x * 2 + y, y * 4 + side * 3
                turn = (8 * (to - at)) % 128
                value = pltpu.roll(code[x], turn, 1) if turn else code[x]
                z_code = jnp.where(element == to, when(inside[4 + side], value, -1.0), z_code)

    for copy in halo:
        copy.wait()

    def halo_rhs(i):
        return stacked(columns_of(slabs[i].reshape(64, 128)))

    def rows_y(k, y):
        return jnp.concatenate([ycat[k, x, y * 64 : y * 64 + 64] for x in range(2)], axis=0)

    def rows_z(k, z):
        return [
            ycat[k, x, y * 64 + z * 16 : y * 64 + z * 16 + 16] for x in range(2) for y in range(2)
        ]

    edges = jnp.concatenate(
        [
            terms(ycat[1, 0], halo_rhs(2), 0),
            terms(ycat[2, 1], halo_rhs(3), 0),
            terms(rows_y(3, 0), halo_rhs(4), 0),
            terms(rows_y(4, 1), halo_rhs(5), 0),
        ],
        axis=0,
    )
    send(1, dot(jnp.concatenate([selection(c) for c in edge_codes], axis=1), edges))
    edges = terms(jnp.concatenate(rows_z(5, 0) + rows_z(6, 3), axis=0), halo_rhs(6), 0)
    edges = dot(selection(z_code), edges)
    send(2, jnp.concatenate([edges[:, :128] + labels, edges[:, 128:]], axis=1))

    per_stage = len(ORDER) + 1

    def arrive(stage):
        for copy in copies[stage * per_stage : stage * per_stage + per_stage - 1]:
            copy.wait()
        copies[stage * per_stage + per_stage - 1].wait()

    def came(stage, h, r):
        return recv[pl.ds(stage * 16 + h * 8 + r, 8, stride=48), :]

    arrive(0)
    for s in range(AGGS):
        for h in range(2):
            out_ref[:, s * 256 + h * 128 : s * 256 + h * 128 + 128] = came(0, h, s)
    arrive(1)
    arrive(2)
    marks = came(2, 0, 4)
    for axis in range(3):
        stage, at = (1, axis * 4) if axis < 2 else (2, 0)
        values = [[came(stage, h, at + p) for h in range(2)] for p in range(4)]
        tags = [
            jnp.broadcast_to(marks[:, axis * 4 + p : axis * 4 + p + 1], (8, 128)) for p in range(4)
        ]
        for column in range(16):
            hits = [tag == column + 1.0 for tag in tags]
            for h in range(2):
                total = jnp.where(hits[0], values[0][h], 0.0)
                for p in range(1, 4):
                    total += jnp.where(hits[p], values[p][h], 0.0)
                at_lane = (AGGS * (1 + 2 * axis) + column) * 256 + h * 128
                out_ref[:, at_lane : at_lane + 128] = total


def solution(mesh):
    sizes = (mesh.shape["gx"], mesh.shape["gy"], mesh.shape["gz"])

    def shards(fine_blocks, prolong, agg_map, owner_map):
        fine = fine_blocks.transpose(0, 1, 3, 2, 4).reshape(2, 2, 7, 4, 32, 128)
        fine = fine.transpose(0, 1, 2, 4, 3, 5).reshape(3584, 128)
        base = prolong.reshape(2, 2, 4, 8, 128).transpose(0, 1, 3, 2, 4)
        inner = len(INNER) * 128
        result = pl.pallas_call(
            functools.partial(kernel, sizes),
            out_shape=jax.ShapeDtypeStruct((AGGS, 7 * AGGS * 256), F32),
            in_specs=[pl.BlockSpec(memory_space=pl.ANY)] * 4,
            out_specs=pl.BlockSpec(memory_space=pltpu.VMEM),
            scratch_shapes=[
                pltpu.VMEM((3584, 128), F32),
                pltpu.VMEM((7, 8, 8, 128), F32),
                pltpu.VMEM((4,) + agg_map.shape[1:], jnp.int32),
                pltpu.VMEM((1, 1, AGGS), jnp.int32),
                pltpu.VMEM((4, 256, 896), BF16),
                pltpu.VMEM((7, 2, 128, 256), BF16),
                pltpu.VMEM((inner, 256), BF16),
                pltpu.VMEM((64, inner), BF16),
                pltpu.VMEM((384, 128), F32),
                pltpu.VMEM((384, 128), F32),
                pltpu.SemaphoreType.DMA((13,)),
                pltpu.SemaphoreType.DMA((16,)),
                pltpu.SemaphoreType.DMA((16,)),
                pltpu.SemaphoreType.DMA((3, 8)),
                pltpu.SemaphoreType.DMA((3, 8)),
                pltpu.SemaphoreType.REGULAR((3,)),
            ],
            compiler_params=pltpu.CompilerParams(collective_id=0, has_side_effects=True),
        )(fine, base, agg_map, owner_map)
        return result.reshape(1, 1, AGGS, 7 * AGGS * 256)

    placed = (P("gx", "gy", "gz", None, None), P("gx", "gy", "gz", None), P(), P("gx", "gy", "gz"))
    return jax.shard_map(
        shards, mesh=mesh, in_specs=placed, out_specs=P("gx", "gy", "gz", None), check_vma=False
    )
```

```python
import functools

import jax
import jax.numpy as jnp
from jax import lax
from jax.experimental import pallas as pl
from jax.experimental.pallas import tpu as pltpu
from jax.sharding import PartitionSpec as P

MESH = pl.DeviceIdType.MESH
F32 = jnp.float32
BF16 = jnp.bfloat16
MEET_AT = 0
AGGS = 8
FACES = 7
STEPS = ((0, 0, 0), (-1, 0, 0), (1, 0, 0), (0, -1, 0), (0, 1, 0), (0, 0, -1), (0, 0, 1))
ORDER = (4, 3, 5, 2, 6, 1, 7)
INNER = tuple((x, k) for x in range(2) for k in range(FACES) if (x, k) not in ((0, 1), (1, 2)))


def iota(shape, dim):
    return lax.broadcasted_iota(jnp.int32, shape, dim)


def split(value):
    high = value.astype(BF16)
    return high, (value - high.astype(F32)).astype(BF16)


def dot(a, b):
    return jnp.dot(a, b, preferred_element_type=F32)


def columns_of(slab):
    row, group = iota((64, 128), 0) & 7, iota((64, 128), 1) >> 4
    for bit in (4, 2, 1):
        row_bit, group_bit = row & bit, group & bit
        down = pltpu.roll(pltpu.roll(slab, 128 - 16 * bit, 1), bit, 0)
        up = pltpu.roll(pltpu.roll(slab, 16 * bit, 1), 64 - bit, 0)
        slab = jnp.where(row_bit == group_bit, slab, jnp.where(row_bit > 0, down, up))
    return slab


def stacked(cols):
    high, low = split(cols)
    return jnp.concatenate([high, low, high, low], axis=0)


def kernel(
    sizes, a_hbm, p_hbm, agg_hbm, own_hbm, recv,
    a_v, slabs, agg_v, own_v, acat, ycat, tcat, scat, msg,
    local_sem, halo_send, halo_recv, send_sem, recv_sem, ready,
):
    nx, ny, nz = sizes
    gx, gy, gz = lax.axis_index("gx"), lax.axis_index("gy"), lax.axis_index("gz")

    def device(dx, dy, dz):
        return (
            lax.rem(gx + dx + nx, nx),
            lax.rem(gy + dy + ny, ny),
            lax.rem(gz + dz + nz, nz),
        )

    def signal(sem, target):
        pl.semaphore_signal(sem, inc=1, device_id=target, device_id_type=MESH)

    inside = (gx > 0, gx < nx - 1, gy > 0, gy < ny - 1, gz > 0, gz < nz - 1)

    barrier = pltpu.get_barrier_semaphore()
    for n, step in enumerate(STEPS[1:]):
        if n < 4:
            pl.when(inside[n])(functools.partial(signal, barrier, device(*step)))
        else:
            signal(barrier, device(*step))

    prolong_copies, fine_copies, index_copies = [], [], []
    for x in range(2):
        for y in range(2):
            c = x * 2 + y
            prolong_copies.append(
                pltpu.make_async_copy(
                    p_hbm.at[x, y], slabs.at[x, :, pl.ds(4 * y, 4), :], local_sem.at[c]
                )
            )
            rows = pl.ds(c * 896, 896)
            fine_copies.append(
                pltpu.make_async_copy(a_hbm.at[rows], a_v.at[rows], local_sem.at[4 + c])
            )
    for plane in range(4):
        where = jnp.clip(gx * 2 - 1 + plane, 0, 2 * nx - 1)
        index_copies.append(
            pltpu.make_async_copy(
                agg_hbm.at[pl.ds(where, 1)], agg_v.at[pl.ds(plane, 1)], local_sem.at[8 + plane]
            )
        )
    index_copies.append(pltpu.make_async_copy(own_hbm, own_v, local_sem.at[12]))
    for copy in prolong_copies + fine_copies + index_copies:
        copy.start()

    halo = [[] for _ in range(6)]
    used = [0]

    def halo_copy(face, src, dst):
        n = used[0]
        used[0] += 1
        halo[face].append(
            pltpu.make_async_remote_copy(
                src_ref=src, dst_ref=dst, send_sem=halo_send.at[n], recv_sem=halo_recv.at[n],
                device_id=device(*STEPS[1 + face]), device_id_type=MESH,
            )
        )

    for u in range(2):
        half = pl.ds(4 * u, 4)
        halo_copy(0, p_hbm.at[0, u], slabs.at[3, :, half, :])
        halo_copy(1, p_hbm.at[1, u], slabs.at[2, :, half, :])
        halo_copy(2, p_hbm.at[u, 0], slabs.at[5, :, half, :])
        halo_copy(3, p_hbm.at[u, 1], slabs.at[4, :, half, :])
        for v in range(2):
            halo_copy(4, p_hbm.at[u, v, :, 0, :], slabs.at[6, :, 4 + u * 2 + v, :])
            halo_copy(5, p_hbm.at[u, v, :, 3, :], slabs.at[6, :, u * 2 + v, :])

    def greet(stage):
        for step in (-1, 1):
            signal(ready.at[stage], device(0, 0, step))

    def meet():
        pl.semaphore_wait(barrier, 2 + sum(flag.astype(jnp.int32) for flag in inside[:4]))
        for face in (2, 3, 4, 5, 0, 1):

            @pl.when(inside[face])
            def _():
                for copy in halo[face]:
                    copy.start()

        greet(0)
        for face in range(4):

            @pl.when(~inside[face])
            def _():
                slabs[2 + face] = jnp.zeros((8, 8, 128), F32)

        for face in (4, 5):

            @pl.when(~inside[face])
            def _():
                slabs[6, :, (face - 4) * 4 : (face - 4) * 4 + 4, :] = jnp.zeros((8, 4, 128), F32)

    for copy in prolong_copies:
        copy.wait()
    own_cols = [columns_of(slabs[x].reshape(64, 128)) for x in range(2)]
    own_rhs = [stacked(cols) for cols in own_cols]
    turned = jnp.concatenate(split(jnp.concatenate(own_cols, axis=0).T), axis=0)
    lane = iota((128, 256), 1)
    spot = 2 * ((lane & 127) >> 2) + (lane >> 7)
    keep = ((iota((256, 256), 0) >> 4) & 3) == (iota((256, 256), 1) & 3)
    left = {}
    for x in range(2):
        spread = (iota((128, 256), 0) == spot + 64 * x).astype(BF16)
        wide = jnp.where(keep, dot(turned, spread), 0.0).astype(BF16)
        for y in range(2):
            parts = []
            for at in (y * 64, 128 + y * 64):
                rows = wide[at : at + 64]
                parts.append(jnp.concatenate([rows[:, :128], rows[:, 128:]], axis=0))
            left[x, y] = parts

    low_lanes = iota((64, 128), 1) < 64
    for x in range(2):
        for y in range(2):
            c = x * 2 + y
            fine_copies[c].wait()
            for k in range(FACES):
                high, low = split(a_v[pl.ds((c * FACES + k) * 128, 128), :])
                acat[c, 0:128, k * 128 : (k + 1) * 128] = high
                acat[c, 128:256, k * 128 : (k + 1) * 128] = low
            high, low = left[x, y]
            both = dot(jnp.concatenate([high, high], axis=1), acat[c]) + dot(low, acat[c, 0:128])
            for k in range(FACES):
                tile = both[:, k * 128 : (k + 1) * 128]
                tile = jnp.where(low_lanes, tile[0:64], tile[64:128])
                tile = tile + pltpu.roll(tile, 64, 1)
                high, low = split(tile)
                ycat[k, x, y * 64 : y * 64 + 64, 0:128] = high
                ycat[k, x, y * 64 : y * 64 + 64, 128:256] = low
            if c == MEET_AT:
                meet()
            if c == 2:
                pl.semaphore_wait(ready.at[0], 2)
                greet(1)
            if c == 3:
                pl.semaphore_wait(ready.at[1], 2)
                greet(2)

    for copy in index_copies:
        copy.wait()
    agg_rows = agg_v[...].reshape(4 * 2 * ny, 4 * nz).astype(F32).astype(BF16)
    shape = (16, 4 * 2 * ny)
    line = iota(shape, 0)
    take = iota(shape, 1) == (line >> 2) * (2 * ny) + gy * 2 - 1 + (line & 3)
    near = dot(take.astype(BF16), agg_rows).astype(BF16)
    shape = (4 * nz, 384)
    lane = iota(shape, 1)
    take = iota(shape, 0) == gz * 4 + ((lane >> 3) & 3) + (lane >> 7) - 1
    near = dot(near, take.astype(BF16))
    lane = iota((1, 128), 1)
    element, z_at, y_high = (lane >> 3) & 7, (lane >> 3) & 3, ((lane >> 5) & 1) == 1

    def slot(x, dx, dy, dz):
        lanes = slice((dz + 1) * 128, (dz + 2) * 128)
        row = (x + 1 + dx) * 4 + 1 + dy
        return jnp.where(y_high, near[row + 1 : row + 2, lanes], near[row : row + 1, lanes])

    slots = [[slot(x, *step) for step in STEPS] for x in range(2)]
    owners = own_v[0].astype(F32)
    owner = [jnp.zeros((1, 128), F32)] * 2
    for s in range(AGGS):
        value = jnp.broadcast_to(owners[:, s : s + 1], (1, 128))
        owner = [jnp.where(slots[x][0] == s, value, owner[x]) for x in range(2)]
    place = [jnp.zeros((1, 128), F32)] * 2
    for m in range(AGGS):
        turn = [pltpu.roll(owner[x], 8 * m, 1) if m else owner[x] for x in range(2)]
        if m:
            for x in range(2):
                place[x] += jnp.where((turn[x] == owner[x]) & (element >= m), 1.0, 0.0)
        place[1] += jnp.where(turn[0] == owner[1], 1.0, 0.0)
    code = [owner[x] * 8.0 + place[x] for x in range(2)]

    row64 = iota((64, 128), 0).astype(F32)

    def selection(codes):
        return (row64 == codes).astype(BF16)

    for n, (x, k) in enumerate(INNER):
        codes = owner[x] * 8.0 + slots[x][k]
        valid = {3: y_high, 4: ~y_high, 5: z_at >= 1, 6: z_at <= 2}.get(k)
        if valid is not None:
            codes = jnp.where(valid, codes, -1.0)
        scat[:, n * 128 : (n + 1) * 128] = selection(codes)

    fold = ((iota((256, 128), 0) & 15) == (iota((256, 128), 1) & 15)).astype(BF16)
    row_e, lane_e = iota((128, 128), 0) >> 4, iota((128, 128), 1) >> 4
    on_c = (iota((128, 128), 0) & 7) == lane_e

    def terms(lhs, rhs, shift):
        block = jnp.where(row_e + shift == lane_e, dot(lhs, rhs), 0.0)
        tall = jnp.where(on_c, dot(jnp.concatenate(split(block), axis=1), fold), 0.0)
        tall = tall.reshape(8, 16, 128)
        tall = jnp.concatenate(
            [tall[:, 0:8].reshape(64, 128), tall[:, 8:16].reshape(64, 128)], axis=1
        )
        return jnp.concatenate(split(tall), axis=0)

    shifts = {3: -4, 4: 4, 5: -1, 6: 1}
    for n, (x, k) in enumerate(INNER):
        other = {1: 0, 2: 1}.get(k, x)
        tcat[n * 128 : (n + 1) * 128, :] = terms(ycat[k, x], own_rhs[other], shifts.get(k, 0))

    copies = []

    def send(stage, rows):
        for o in range(AGGS):
            for h in range(2):
                msg[pl.ds(o * 48 + stage * 16 + h * 8, 8), :] = rows[
                    o * 8 : o * 8 + 8, h * 128 : (h + 1) * 128
                ]
        target_rows = pl.ds(pl.multiple_of(gz * 48 + stage * 16, 16), 16)
        for d in ORDER:
            target = device(0, 0, d)
            copy = pltpu.make_async_remote_copy(
                src_ref=msg.at[pl.ds(pl.multiple_of(target[2] * 48 + stage * 16, 16), 16)],
                dst_ref=recv.at[target_rows],
                send_sem=send_sem.at[stage, d], recv_sem=recv_sem.at[stage, d],
                device_id=target, device_id_type=MESH,
            )
            copy.start()
            copies.append(copy)
        copy = pltpu.make_async_copy(
            msg.at[target_rows], recv.at[target_rows], recv_sem.at[stage, 0]
        )
        copy.start()
        copies.append(copy)

    pl.semaphore_wait(ready.at[2], 2)
    send(0, dot(scat[...], tcat[...]))

    def when(flag, value, other):
        return jnp.where(jnp.full((1, 128), flag), value, other)

    label = [
        [
            when(inside[0], slots[0][1] + 1.0, 0.0),
            when(inside[1], slots[1][2] + 9.0, 0.0),
        ],
        [
            jnp.where(
                y_high,
                when(inside[3], slots[x][4] + 9.0, 0.0),
                when(inside[2], slots[x][3] + 1.0, 0.0),
            )
            for x in range(2)
        ],
        [
            jnp.where(
                z_at == 0,
                when(inside[4], slots[x][5] + 1.0, 0.0),
                jnp.where(z_at == 3, when(inside[5], slots[x][6] + 9.0, 0.0), 0.0),
            )
            for x in range(2)
        ],
    ]
    row, lane_all = iota((128, 128), 0), iota((128, 128), 1)
    once = ((lane_all & 7) == 0) & (lane_all < 64)
    which, who = [], []
    for x in range(2):
        value = jnp.where(
            row < 4, label[0][x], jnp.where(row < 8, label[1][x], jnp.where(row < 12, label[2][x], 0.0))
        )
        value = jnp.where(once & ((row & 3).astype(F32) == place[x]), value, 0.0)
        which.append(value.astype(BF16))
        row_o = iota((64, 128), 0)
        who.append((((row_o & 7) == 4) & ((row_o >> 3).astype(F32) == owner[x])).astype(BF16))
    labels = lax.dot_general(
        jnp.concatenate(who, axis=1), jnp.concatenate(which, axis=1),
        (((1,), (1,)), ((), ())), preferred_element_type=F32,
    )

    edge_codes = [
        code[0],
        code[1],
        jnp.where(y_high, pltpu.roll(code[1], 32, 1), code[0]) + 4.0,
        jnp.where(y_high, code[1], pltpu.roll(code[0], 96, 1)) + 4.0,
    ]
    edge_codes = [when(inside[i], edge_codes[i], -1.0) for i in range(4)]
    z_code = jnp.full((1, 128), -1.0, F32)
    for side in range(2):
        for x in range(2):
            for y in range(2):
                to, at = side * 4 + x * 2 + y, y * 4 + side * 3
                turn = (8 * (to - at)) % 128
                value = pltpu.roll(code[x], turn, 1) if turn else code[x]
                z_code = jnp.where(element == to, when(inside[4 + side], value, -1.0), z_code)

    for face in range(6):

        @pl.when(inside[face])
        def _():
            for mine, theirs in zip(halo[face], halo[face ^ 1]):
                mine.wait_send()
                theirs.wait_recv()

    def halo_rhs(i):
        return stacked(columns_of(slabs[i].reshape(64, 128)))

    def rows_y(k, y):
        return jnp.concatenate([ycat[k, x, y * 64 : y * 64 + 64] for x in range(2)], axis=0)

    def rows_z(k, z):
        return [
            ycat[k, x, y * 64 + z * 16 : y * 64 + z * 16 + 16] for x in range(2) for y in range(2)
        ]

    edges = jnp.concatenate(
        [
            terms(ycat[1, 0], halo_rhs(2), 0),
            terms(ycat[2, 1], halo_rhs(3), 0),
            terms(rows_y(3, 0), halo_rhs(4), 0),
            terms(rows_y(4, 1), halo_rhs(5), 0),
        ],
        axis=0,
    )
    send(1, dot(jnp.concatenate([selection(c) for c in edge_codes], axis=1), edges))
    edges = terms(jnp.concatenate(rows_z(5, 0) + rows_z(6, 3), axis=0), halo_rhs(6), 0)
    edges = dot(selection(z_code), edges)
    send(2, jnp.concatenate([edges[:, :128] + labels, edges[:, 128:]], axis=1))

    for copy in copies:
        copy.wait()


def spread(recv, out_ref):
    def came(stage, h, r):
        return recv[pl.ds(stage * 16 + h * 8 + r, 8, stride=48), :]

    for s in range(AGGS):
        for h in range(2):
            out_ref[:, s * 256 + h * 128 : s * 256 + h * 128 + 128] = came(0, h, s)
    marks = came(2, 0, 4)
    for axis in range(3):
        stage, at = (1, axis * 4) if axis < 2 else (2, 0)
        values = [[came(stage, h, at + p) for h in range(2)] for p in range(4)]
        tags = [
            jnp.broadcast_to(marks[:, axis * 4 + p : axis * 4 + p + 1], (8, 128)) for p in range(4)
        ]
        for column in range(16):
            hits = [tag == column + 1.0 for tag in tags]
            for h in range(2):
                total = jnp.where(hits[0], values[0][h], 0.0)
                for p in range(1, 4):
                    total += jnp.where(hits[p], values[p][h], 0.0)
                at_lane = (AGGS * (1 + 2 * axis) + column) * 256 + h * 128
                out_ref[:, at_lane : at_lane + 128] = total


def solution(mesh):
    sizes = (mesh.shape["gx"], mesh.shape["gy"], mesh.shape["gz"])

    def shards(fine_blocks, prolong, agg_map, owner_map):
        fine = fine_blocks.transpose(0, 1, 3, 2, 4).reshape(2, 2, 7, 4, 32, 128)
        fine = fine.transpose(0, 1, 2, 4, 3, 5).reshape(3584, 128)
        base = prolong.reshape(2, 2, 4, 8, 128).transpose(0, 1, 3, 2, 4)
        inner = len(INNER) * 128
        rows = pl.pallas_call(
            functools.partial(kernel, sizes),
            out_shape=jax.ShapeDtypeStruct((384, 128), F32),
            in_specs=[pl.BlockSpec(memory_space=pl.ANY)] * 4,
            out_specs=pl.BlockSpec(memory_space=pltpu.VMEM),
            scratch_shapes=[
                pltpu.VMEM((3584, 128), F32),
                pltpu.VMEM((7, 8, 8, 128), F32),
                pltpu.VMEM((4,) + agg_map.shape[1:], jnp.int32),
                pltpu.VMEM((1, 1, AGGS), jnp.int32),
                pltpu.VMEM((4, 256, 896), BF16),
                pltpu.VMEM((7, 2, 128, 256), BF16),
                pltpu.VMEM((inner, 256), BF16),
                pltpu.VMEM((64, inner), BF16),
                pltpu.VMEM((384, 128), F32),
                pltpu.SemaphoreType.DMA((13,)),
                pltpu.SemaphoreType.DMA((16,)),
                pltpu.SemaphoreType.DMA((16,)),
                pltpu.SemaphoreType.DMA((3, 8)),
                pltpu.SemaphoreType.DMA((3, 8)),
                pltpu.SemaphoreType.REGULAR((3,)),
            ],
            compiler_params=pltpu.CompilerParams(collective_id=0, has_side_effects=True),
        )(fine, base, agg_map, owner_map)
        result = pl.pallas_call(
            spread,
            out_shape=jax.ShapeDtypeStruct((AGGS, 7 * AGGS * 256), F32),
            in_specs=[pl.BlockSpec(memory_space=pltpu.VMEM)],
            out_specs=pl.BlockSpec(memory_space=pltpu.VMEM),
        )(rows)
        return result.reshape(1, 1, AGGS, 7 * AGGS * 256)

    placed = (P("gx", "gy", "gz", None, None), P("gx", "gy", "gz", None), P(), P("gx", "gy", "gz"))
    return jax.shard_map(
        shards, mesh=mesh, in_specs=placed, out_specs=P("gx", "gy", "gz", None), check_vma=False
    )
```

```python
import functools

import jax
import jax.numpy as jnp
from jax import lax
from jax.experimental import pallas as pl
from jax.experimental.pallas import tpu as pltpu
from jax.sharding import PartitionSpec as P

MESH = pl.DeviceIdType.MESH
F32 = jnp.float32
BF16 = jnp.bfloat16
AGGS = 8
FACES = 7
STEPS = ((0, 0, 0), (-1, 0, 0), (1, 0, 0), (0, -1, 0), (0, 1, 0), (0, 0, -1), (0, 0, 1))


def iota(shape, dim):
    return lax.broadcasted_iota(jnp.int32, shape, dim)


def split(value):
    high = value.astype(BF16)
    return high, (value - high.astype(F32)).astype(BF16)


def dot(a, b):
    return jnp.dot(a, b, preferred_element_type=F32)


def columns_of(slab):
    row, group = iota((8, 8, 128), 1), iota((8, 8, 128), 2) >> 4
    for bit in (4, 2, 1):
        row_bit, group_bit = row & bit, group & bit
        down = pltpu.roll(pltpu.roll(slab, 128 - 16 * bit, 2), bit, 1)
        if bit == 4:
            slab = jnp.where(row_bit == group_bit, slab, down)
        else:
            up = pltpu.roll(pltpu.roll(slab, 16 * bit, 2), 8 - bit, 1)
            slab = jnp.where(row_bit == group_bit, slab, jnp.where(row_bit > 0, down, up))
    return slab.reshape(64, 128)


def stacked(cols):
    high, low = split(cols)
    return jnp.concatenate([high, low, high, low], axis=0)


def kernel(
    sizes, a_hbm, p_hbm, agg_hbm, own_hbm, recv,
    a_v, slabs, agg_v, own_v, yv, msg,
    local_sem, halo_send, halo_recv, row_send, row_recv, ready,
):
    nx, ny, nz = sizes
    gx, gy, gz = lax.axis_index("gx"), lax.axis_index("gy"), lax.axis_index("gz")

    def device(dx, dy, dz):
        return (
            lax.rem(gx + dx + nx, nx),
            lax.rem(gy + dy + ny, ny),
            lax.rem(gz + dz + nz, nz),
        )

    def signal(sem, target):
        pl.semaphore_signal(sem, inc=1, device_id=target, device_id_type=MESH)

    inside = (gx > 0, gx < nx - 1, gy > 0, gy < ny - 1, gz > 0, gz < nz - 1)

    barrier = pltpu.get_barrier_semaphore()
    for n, step in enumerate(STEPS[1:]):
        if n < 4:
            pl.when(inside[n])(functools.partial(signal, barrier, device(*step)))
        else:
            signal(barrier, device(*step))

    def copied(dst, n):
        return pltpu.make_async_copy(dst, dst, local_sem.at[n])

    for x in range(2):
        for y in range(2):
            half = pl.ds(4 * y, 4)
            pltpu.make_async_copy(
                p_hbm.at[x, y], slabs.at[x, :, half, :], local_sem.at[0]
            ).start()
    for c in range(4):
        rows = pl.ds(c * 896, 896)
        pltpu.make_async_copy(a_hbm.at[rows], a_v.at[rows], local_sem.at[1]).start()
    for plane in range(4):
        where = jnp.clip(gx * 2 - 1 + plane, 0, 2 * nx - 1)
        pltpu.make_async_copy(
            agg_hbm.at[pl.ds(where, 1)], agg_v.at[pl.ds(plane, 1)], local_sem.at[2]
        ).start()
    pltpu.make_async_copy(own_hbm, own_v, local_sem.at[3]).start()

    halo = [[] for _ in range(6)]

    def halo_copy(face, src, dst):
        halo[face].append(
            pltpu.make_async_remote_copy(
                src_ref=src, dst_ref=dst,
                send_sem=halo_send.at[face], recv_sem=halo_recv.at[face],
                device_id=device(*STEPS[1 + face]), device_id_type=MESH,
            )
        )

    for u in range(2):
        half = pl.ds(4 * u, 4)
        halo_copy(0, p_hbm.at[0, u], slabs.at[3, :, half, :])
        halo_copy(1, p_hbm.at[1, u], slabs.at[2, :, half, :])
        halo_copy(2, p_hbm.at[u, 0], slabs.at[5, :, half, :])
        halo_copy(3, p_hbm.at[u, 1], slabs.at[4, :, half, :])
        for v in range(2):
            halo_copy(4, p_hbm.at[u, v, :, 0, :], slabs.at[6, :, 4 + u * 2 + v, :])
            halo_copy(5, p_hbm.at[u, v, :, 3, :], slabs.at[6, :, u * 2 + v, :])

    def halo_wait(face):
        slab = slabs.at[2 + face] if face < 4 else slabs.at[6, :, pl.ds((face - 4) * 4, 4), :]
        done = pltpu.make_async_remote_copy(
            src_ref=slab, dst_ref=slab,
            send_sem=halo_send.at[face], recv_sem=halo_recv.at[face ^ 1],
            device_id=device(*STEPS[1 + face]), device_id_type=MESH,
        )
        done.wait_send()
        done.wait_recv()

    def tell(stage):
        for step in (-1, 1):
            signal(ready.at[stage], device(0, 0, step))

    def learn(stage):
        pl.semaphore_wait(ready.at[stage], 2)
        if stage < 2:
            tell(stage + 1)

    def meet():
        pl.semaphore_wait(barrier, 2 + sum(flag.astype(jnp.int32) for flag in inside[:4]))
        for face in (2, 3, 4, 5, 0, 1):

            @pl.when(inside[face])
            def _():
                for copy in halo[face]:
                    copy.start()

        tell(0)
        for face in range(4):

            @pl.when(~inside[face])
            def _():
                slabs[2 + face] = jnp.zeros((8, 8, 128), F32)

        for face in (4, 5):

            @pl.when(~inside[face])
            def _():
                slabs[6, :, (face - 4) * 4 : (face - 4) * 4 + 4, :] = jnp.zeros((8, 4, 128), F32)

    copied(slabs.at[pl.ds(0, 2)], 0).wait()
    own_cols = [columns_of(slabs[x]) for x in range(2)]
    own_rhs = [stacked(cols) for cols in own_cols]
    turned = jnp.concatenate(split(jnp.concatenate(own_cols, axis=0).T), axis=0)
    lane = iota((128, 256), 1)
    spot = 2 * ((lane & 127) >> 2) + (lane >> 7)
    keep = ((iota((256, 256), 0) >> 4) & 3) == (iota((256, 256), 1) & 3)
    left = {}
    for x in range(2):
        spread = (iota((128, 256), 0) == spot + 64 * x).astype(BF16)
        wide = jnp.where(keep, dot(turned, spread), 0.0).astype(BF16)
        for y in range(2):
            parts = []
            for at in (y * 64, 128 + y * 64):
                rows = wide[at : at + 64]
                parts.append(jnp.concatenate([rows[:, :128], rows[:, 128:]], axis=0))
            left[x, y] = parts

    meet()

    low_lanes = iota((64, 128), 1) < 64
    copied(a_v, 1).wait()
    for x in range(2):
        for y in range(2):
            c = x * 2 + y
            blocks = [split(a_v[pl.ds((c * FACES + k) * 128, 128), :]) for k in range(FACES)]
            highs = jnp.concatenate([block[0] for block in blocks], axis=1)
            lows = jnp.concatenate([block[1] for block in blocks], axis=1)
            high, low = left[x, y]
            stack = jnp.concatenate([high, low], axis=0)
            both = dot(
                jnp.concatenate([stack, stack], axis=1), jnp.concatenate([highs, lows], axis=0)
            )
            for k in range(FACES):
                tile = both[:, k * 128 : (k + 1) * 128]
                tile = jnp.where(low_lanes, tile[0:64] + tile[128:192], tile[64:128] + tile[192:256])
                yv[k, x, y * 64 : y * 64 + 64, :] = tile + pltpu.roll(tile, 64, 1)
    learn(0)

    copied(agg_v, 2).wait()
    copied(own_v, 3).wait()
    agg_rows = agg_v[...].reshape(4 * 2 * ny, 4 * nz).astype(F32).astype(BF16)
    shape = (16, 4 * 2 * ny)
    line = iota(shape, 0)
    take = iota(shape, 1) == (line >> 2) * (2 * ny) + gy * 2 - 1 + (line & 3)
    near = dot(take.astype(BF16), agg_rows).astype(BF16)
    shape = (4 * nz, 384)
    lane = iota(shape, 1)
    take = iota(shape, 0) == gz * 4 + ((lane >> 3) & 3) + (lane >> 7) - 1
    near = dot(near, take.astype(BF16))
    lane = iota((1, 128), 1)
    element, z_at, y_high = (lane >> 3) & 7, (lane >> 3) & 3, ((lane >> 5) & 1) == 1

    def slot(x, dx, dy, dz):
        lanes = slice((dz + 1) * 128, (dz + 2) * 128)
        row = (x + 1 + dx) * 4 + 1 + dy
        return jnp.where(y_high, near[row + 1 : row + 2, lanes], near[row : row + 1, lanes])

    slots = [[slot(x, *step) for step in STEPS] for x in range(2)]
    owners = own_v[0].astype(F32)
    owner = [jnp.zeros((1, 128), F32)] * 2
    for s in range(AGGS):
        value = jnp.broadcast_to(owners[:, s : s + 1], (1, 128))
        owner = [jnp.where(slots[x][0] == s, value, owner[x]) for x in range(2)]
    place = [jnp.zeros((1, 128), F32)] * 2
    for m in range(AGGS):
        turn = [pltpu.roll(owner[x], 8 * m, 1) if m else owner[x] for x in range(2)]
        if m:
            for x in range(2):
                place[x] += jnp.where((turn[x] == owner[x]) & (element >= m), 1.0, 0.0)
        place[1] += jnp.where(turn[0] == owner[1], 1.0, 0.0)
    code = [owner[x] * 8.0 + place[x] for x in range(2)]

    row64 = iota((64, 128), 0).astype(F32)

    def selection(codes):
        return (row64 == codes).astype(BF16)

    fold = ((iota((256, 128), 0) & 15) == (iota((256, 128), 1) & 15)).astype(BF16)
    group = iota((16, 128), 1) >> 4

    def terms(lhs, rhs, partners, places=tuple(range(8))):
        count = len(partners)
        block = dot(jnp.concatenate(split(lhs), axis=1), rhs)
        block = jnp.concatenate(
            [
                jnp.where(group == partner, block[i * 16 : i * 16 + 16], 0.0)
                for i, partner in enumerate(partners)
            ],
            axis=0,
        )
        tall = dot(jnp.concatenate(split(block), axis=1), fold).reshape(count * 2, 8, 128)
        on_c = iota((count * 2, 8, 128), 1) == (iota((count * 2, 8, 128), 2) >> 4)
        tall = jnp.where(on_c, tall, 0.0).reshape(count, 2, 8, 128)
        rows = [jnp.zeros((8, 256), F32)] * 8
        for i, at in enumerate(places):
            rows[at] = jnp.concatenate([tall[i, 0], tall[i, 1]], axis=1)
        return jnp.concatenate(split(jnp.concatenate(rows, axis=0)), axis=0)

    own = tuple(range(8))
    z_odd = (z_at & 1) == 1
    inner_rows = jnp.zeros((64, 256), F32)
    for x in range(2):
        y = [yv[k, x] for k in range(FACES)]
        at = [[y[k][e * 16 : e * 16 + 16] for e in range(8)] for k in (5, 6)]
        cross = 2 - x
        tiles = [
            (y[0], own_rhs[x], own, own, slots[x][0]),
            (y[cross], own_rhs[1 - x], own, own, slots[x][cross]),
            (
                jnp.concatenate([y[4][:64], y[3][64:]], axis=0), own_rhs[x],
                tuple(e ^ 4 for e in own), own, jnp.where(y_high, slots[x][3], slots[x][4]),
            ),
            (
                jnp.concatenate([at[1 - (e & 1)][e] for e in own], axis=0), own_rhs[x],
                tuple(e ^ 1 for e in own), own, jnp.where(z_odd, slots[x][5], slots[x][6]),
            ),
            (
                jnp.concatenate([at[e & 1][e] for e in (1, 2, 5, 6)], axis=0), own_rhs[x],
                (2, 1, 6, 5), (1, 2, 5, 6),
                jnp.where(
                    z_at == 1, slots[x][6], jnp.where(z_at == 2, slots[x][5], -1000.0)
                ),
            ),
        ]
        for lhs, rhs, partners, places, column in tiles:
            inner_rows += dot(selection(owner[x] * 8.0 + column), terms(lhs, rhs, partners, places))

    def put(at, rows):
        for o in range(AGGS):
            for h in range(2):
                msg[pl.ds(o * 48 + at + h * 8, 8), :] = rows[
                    o * 8 : o * 8 + 8, h * 128 : (h + 1) * 128
                ]

    def rows_of(device_at, at, count):
        return pl.ds(pl.multiple_of(device_at * 48 + at, 16), count)

    def send(d, at, count):
        target = device(0, 0, d)
        pltpu.make_async_remote_copy(
            src_ref=msg.at[rows_of(target[2], at, count)],
            dst_ref=recv.at[rows_of(gz, at, count)],
            send_sem=row_send.at[0], recv_sem=row_recv.at[0],
            device_id=target, device_id_type=MESH,
        ).start()

    put(0, inner_rows)
    learn(1)
    for d in (1, -1, 2, -2, 3, -3):
        send(d, 0, 16)

    def when(flag, value, other):
        return jnp.where(jnp.full((1, 128), flag), value, other)

    label = [
        [
            when(inside[0], slots[0][1] + 1.0, 0.0),
            when(inside[1], slots[1][2] + 9.0, 0.0),
        ],
        [
            jnp.where(
                y_high,
                when(inside[3], slots[x][4] + 9.0, 0.0),
                when(inside[2], slots[x][3] + 1.0, 0.0),
            )
            for x in range(2)
        ],
        [
            jnp.where(
                z_at == 0,
                when(inside[4], slots[x][5] + 1.0, 0.0),
                jnp.where(z_at == 3, when(inside[5], slots[x][6] + 9.0, 0.0), 0.0),
            )
            for x in range(2)
        ],
    ]
    row, lane_all = iota((128, 128), 0), iota((128, 128), 1)
    once = ((lane_all & 7) == 0) & (lane_all < 64)
    which, who = [], []
    for x in range(2):
        value = jnp.where(
            row < 4, label[0][x], jnp.where(row < 8, label[1][x], jnp.where(row < 12, label[2][x], 0.0))
        )
        value = jnp.where(once & ((row & 3).astype(F32) == place[x]), value, 0.0)
        which.append(value.astype(BF16))
        row_o = iota((64, 128), 0)
        who.append((((row_o & 7) == 4) & ((row_o >> 3).astype(F32) == owner[x])).astype(BF16))
    labels = lax.dot_general(
        jnp.concatenate(who, axis=1), jnp.concatenate(which, axis=1),
        (((1,), (1,)), ((), ())), preferred_element_type=F32,
    )

    edge_codes = [
        code[0],
        code[1],
        jnp.where(y_high, pltpu.roll(code[1], 32, 1), code[0]) + 4.0,
        jnp.where(y_high, code[1], pltpu.roll(code[0], 96, 1)) + 4.0,
    ]
    edge_codes = [when(inside[i], edge_codes[i], -1.0) for i in range(4)]
    z_code = jnp.full((1, 128), -1.0, F32)
    for side in range(2):
        for x in range(2):
            for y in range(2):
                to, at = side * 4 + x * 2 + y, y * 4 + side * 3
                turn = (8 * (to - at)) % 128
                value = pltpu.roll(code[x], turn, 1) if turn else code[x]
                z_code = jnp.where(element == to, when(inside[4 + side], value, -1.0), z_code)

    for face in range(6):
        pl.when(inside[face])(functools.partial(halo_wait, face))

    def halo_rhs(i):
        return stacked(columns_of(slabs[i]))

    def rows_y(k, y):
        return jnp.concatenate([yv[k, x, y * 64 : y * 64 + 64] for x in range(2)], axis=0)

    def rows_z(k, z):
        return [
            yv[k, x, y * 64 + z * 16 : y * 64 + z * 16 + 16] for x in range(2) for y in range(2)
        ]

    sides = [yv[1, 0], yv[2, 1], rows_y(3, 0), rows_y(4, 1)]
    edges = sum(
        dot(selection(edge_codes[i]), terms(sides[i], halo_rhs(2 + i), own)) for i in range(4)
    )
    put(16, edges)
    ends = jnp.concatenate(rows_z(5, 0) + rows_z(6, 3), axis=0)
    edges = dot(selection(z_code), terms(ends, halo_rhs(6), own))
    put(32, jnp.concatenate([edges[:, :128] + labels, edges[:, 128:]], axis=1))

    learn(2)
    for d in (1, -1, 2, -2, 3, -3):
        send(d, 16, 32)
    send(4, 0, 48)
    stay = pltpu.make_async_copy(
        msg.at[rows_of(gz, 0, 48)], recv.at[rows_of(gz, 0, 48)], local_sem.at[0]
    )
    stay.start()

    others = pltpu.make_async_remote_copy(
        src_ref=msg.at[pl.ds(0, 336)], dst_ref=recv.at[pl.ds(0, 336)],
        send_sem=row_send.at[0], recv_sem=row_recv.at[0],
        device_id=device(0, 0, 1), device_id_type=MESH,
    )
    others.wait_send()
    others.wait_recv()
    stay.wait()


def spread(recv, out_ref):
    def came(stage, h, r):
        return recv[pl.ds(stage * 16 + h * 8 + r, 8, stride=48), :]

    for s in range(AGGS):
        for h in range(2):
            out_ref[:, s * 256 + h * 128 : s * 256 + h * 128 + 128] = came(0, h, s)
    marks = came(2, 0, 4)
    for axis in range(3):
        stage, at = (1, axis * 4) if axis < 2 else (2, 0)
        values = [[came(stage, h, at + p) for h in range(2)] for p in range(4)]
        tags = [
            jnp.broadcast_to(marks[:, axis * 4 + p : axis * 4 + p + 1], (8, 128)) for p in range(4)
        ]
        for column in range(16):
            hits = [tag == column + 1.0 for tag in tags]
            for h in range(2):
                total = jnp.where(hits[0], values[0][h], 0.0)
                for p in range(1, 4):
                    total += jnp.where(hits[p], values[p][h], 0.0)
                at_lane = (AGGS * (1 + 2 * axis) + column) * 256 + h * 128
                out_ref[:, at_lane : at_lane + 128] = total


def solution(mesh):
    sizes = (mesh.shape["gx"], mesh.shape["gy"], mesh.shape["gz"])

    def shards(fine_blocks, prolong, agg_map, owner_map):
        fine = fine_blocks.transpose(0, 1, 3, 2, 4).reshape(2, 2, 7, 4, 32, 128)
        fine = fine.transpose(0, 1, 2, 4, 3, 5).reshape(3584, 128)
        base = prolong.reshape(2, 2, 4, 8, 128).transpose(0, 1, 3, 2, 4)
        fine, base, agg_map, owner_map = (
            pltpu.with_memory_space_constraint(value, pltpu.HBM)
            for value in (fine, base, agg_map, owner_map)
        )
        rows = pl.pallas_call(
            functools.partial(kernel, sizes),
            out_shape=jax.ShapeDtypeStruct((384, 128), F32),
            in_specs=[pl.BlockSpec(memory_space=pltpu.HBM)] * 4,
            out_specs=pl.BlockSpec(memory_space=pltpu.VMEM),
            scratch_shapes=[
                pltpu.VMEM((3584, 128), F32),
                pltpu.VMEM((7, 8, 8, 128), F32),
                pltpu.VMEM((4,) + agg_map.shape[1:], jnp.int32),
                pltpu.VMEM((1, 1, AGGS), jnp.int32),
                pltpu.VMEM((FACES, 2, 128, 128), F32),
                pltpu.VMEM((384, 128), F32),
                pltpu.SemaphoreType.DMA((4,)),
                pltpu.SemaphoreType.DMA((6,)),
                pltpu.SemaphoreType.DMA((6,)),
                pltpu.SemaphoreType.DMA((1,)),
                pltpu.SemaphoreType.DMA((1,)),
                pltpu.SemaphoreType.REGULAR((3,)),
            ],
            compiler_params=pltpu.CompilerParams(
                collective_id=0, has_side_effects=True, vmem_limit_bytes=16 << 20
            ),
        )(fine, base, agg_map, owner_map)
        result = pl.pallas_call(
            spread,
            out_shape=jax.ShapeDtypeStruct((AGGS, 7 * AGGS * 256), F32),
            in_specs=[pl.BlockSpec(memory_space=pltpu.VMEM)],
            out_specs=pl.BlockSpec(memory_space=pltpu.VMEM),
            compiler_params=pltpu.CompilerParams(vmem_limit_bytes=8 << 20),
        )(rows)
        return result.reshape(1, 1, AGGS, 7 * AGGS * 256)

    placed = (P("gx", "gy", "gz", None, None), P("gx", "gy", "gz", None), P(), P("gx", "gy", "gz"))
    return jax.shard_map(
        shards, mesh=mesh, in_specs=placed, out_specs=P("gx", "gy", "gz", None), check_vma=False
    )
```

```python
import functools

import jax
import jax.numpy as jnp
from jax import lax
from jax.experimental import pallas as pl
from jax.experimental.pallas import tpu as pltpu
from jax.sharding import PartitionSpec as P

MESH = pl.DeviceIdType.MESH
F32 = jnp.float32
BF16 = jnp.bfloat16
AGGS = 8
FACES = 7
STEPS = ((0, 0, 0), (-1, 0, 0), (1, 0, 0), (0, -1, 0), (0, 1, 0), (0, 0, -1), (0, 0, 1))


def iota(shape, dim):
    return lax.broadcasted_iota(jnp.int32, shape, dim)


def split(value):
    high = value.astype(BF16)
    return high, (value - high.astype(F32)).astype(BF16)


def dot(a, b):
    return jnp.dot(a, b, preferred_element_type=F32)


def columns_of(slab):
    row, group = iota((8, 8, 128), 1), iota((8, 8, 128), 2) >> 4
    for bit in (4, 2, 1):
        row_bit, group_bit = row & bit, group & bit
        down = pltpu.roll(pltpu.roll(slab, 128 - 16 * bit, 2), bit, 1)
        if bit == 4:
            slab = jnp.where(row_bit == group_bit, slab, down)
        else:
            up = pltpu.roll(pltpu.roll(slab, 16 * bit, 2), 8 - bit, 1)
            slab = jnp.where(row_bit == group_bit, slab, jnp.where(row_bit > 0, down, up))
    return slab.reshape(64, 128)


def stacked(cols):
    high, low = split(cols)
    return jnp.concatenate([high, low, high, low], axis=0)


def kernel(
    sizes, a_hbm, p_hbm, agg_hbm, own_hbm, recv,
    a_v, slabs, agg_v, own_v, yv, msg,
    local_sem, halo_send, halo_recv, row_send, row_recv, ready,
):
    nx, ny, nz = sizes
    gx, gy, gz = lax.axis_index("gx"), lax.axis_index("gy"), lax.axis_index("gz")

    def device(dx, dy, dz):
        return (
            lax.rem(gx + dx + nx, nx),
            lax.rem(gy + dy + ny, ny),
            lax.rem(gz + dz + nz, nz),
        )

    def signal(sem, target):
        pl.semaphore_signal(sem, inc=1, device_id=target, device_id_type=MESH)

    inside = (gx > 0, gx < nx - 1, gy > 0, gy < ny - 1, gz > 0, gz < nz - 1)

    def copied(dst, n):
        return pltpu.make_async_copy(dst, dst, local_sem.at[n])

    for x in range(2):
        for y in range(2):
            half = pl.ds(4 * y, 4)
            pltpu.make_async_copy(
                p_hbm.at[x, y], slabs.at[x, :, half, :], local_sem.at[0]
            ).start()
    for c in range(4):
        rows = pl.ds(c * 896, 896)
        pltpu.make_async_copy(a_hbm.at[rows], a_v.at[rows], local_sem.at[1]).start()
    for plane in range(4):
        where = jnp.clip(gx * 2 - 1 + plane, 0, 2 * nx - 1)
        pltpu.make_async_copy(
            agg_hbm.at[pl.ds(where, 1)], agg_v.at[pl.ds(plane, 1)], local_sem.at[2]
        ).start()
    pltpu.make_async_copy(own_hbm, own_v, local_sem.at[3]).start()

    barrier = pltpu.get_barrier_semaphore()
    for n, step in enumerate(STEPS[1:]):
        if n < 4:
            pl.when(inside[n])(functools.partial(signal, barrier, device(*step)))
        else:
            signal(barrier, device(*step))

    halo = [[] for _ in range(6)]

    def halo_copy(face, src, dst):
        halo[face].append(
            pltpu.make_async_remote_copy(
                src_ref=src, dst_ref=dst,
                send_sem=halo_send.at[face], recv_sem=halo_recv.at[face],
                device_id=device(*STEPS[1 + face]), device_id_type=MESH,
            )
        )

    for u in range(2):
        half = pl.ds(4 * u, 4)
        halo_copy(0, p_hbm.at[0, u], slabs.at[3, :, half, :])
        halo_copy(1, p_hbm.at[1, u], slabs.at[2, :, half, :])
        halo_copy(2, p_hbm.at[u, 0], slabs.at[5, :, half, :])
        halo_copy(3, p_hbm.at[u, 1], slabs.at[4, :, half, :])
        for v in range(2):
            halo_copy(4, p_hbm.at[u, v, :, 0, :], slabs.at[6, :, 4 + u * 2 + v, :])
            halo_copy(5, p_hbm.at[u, v, :, 3, :], slabs.at[6, :, u * 2 + v, :])

    def halo_wait(face):
        slab = slabs.at[2 + face] if face < 4 else slabs.at[6, :, pl.ds((face - 4) * 4, 4), :]
        done = pltpu.make_async_remote_copy(
            src_ref=slab, dst_ref=slab,
            send_sem=halo_send.at[face], recv_sem=halo_recv.at[face ^ 1],
            device_id=device(*STEPS[1 + face]), device_id_type=MESH,
        )
        done.wait_send()
        done.wait_recv()

    past = {1: lax.rem(nz - gz, nz), -1: gz}
    ways = ((0, 1), (1, -1))

    def late(way, d):
        return (past[way] >= 1) & (past[way] <= d)

    def learn(stage, last):
        for n, way in ways:
            flag = late(way, stage + 2)

            @pl.when(flag if last else ~flag)
            def _():
                pl.semaphore_wait(ready.at[n, stage], 1)
                if stage < 2:
                    signal(ready.at[n, stage + 1], device(0, 0, -way))

    def meet():
        pl.semaphore_wait(barrier, 2 + sum(flag.astype(jnp.int32) for flag in inside[:4]))
        for face in (2, 3, 4, 5, 0, 1):

            @pl.when(inside[face])
            def _():
                for copy in halo[face]:
                    copy.start()

        for n, way in ways:
            signal(ready.at[n, 0], device(0, 0, -way))
        for face in range(4):

            @pl.when(~inside[face])
            def _():
                slabs[2 + face] = jnp.zeros((8, 8, 128), F32)

        for face in (4, 5):

            @pl.when(~inside[face])
            def _():
                slabs[6, :, (face - 4) * 4 : (face - 4) * 4 + 4, :] = jnp.zeros((8, 4, 128), F32)

    meet()

    copied(slabs.at[pl.ds(0, 2)], 0).wait()
    own_cols = [columns_of(slabs[x]) for x in range(2)]
    own_rhs = [stacked(cols) for cols in own_cols]
    turned = jnp.concatenate(split(jnp.concatenate(own_cols, axis=0).T), axis=0)
    lane = iota((128, 256), 1)
    spot = 2 * ((lane & 127) >> 2) + (lane >> 7)
    keep = ((iota((256, 256), 0) >> 4) & 3) == (iota((256, 256), 1) & 3)
    left = {}
    for x in range(2):
        spread = (iota((128, 256), 0) == spot + 64 * x).astype(BF16)
        wide = jnp.where(keep, dot(turned, spread), 0.0).astype(BF16)
        for y in range(2):
            parts = []
            for at in (y * 64, 128 + y * 64):
                rows = wide[at : at + 64]
                parts.append(jnp.concatenate([rows[:, :128], rows[:, 128:]], axis=0))
            left[x, y] = parts

    low_lanes = iota((64, 128), 1) < 64
    learn(0, False)
    copied(a_v, 1).wait()
    for x in range(2):
        for y in range(2):
            c = x * 2 + y
            blocks = [split(a_v[pl.ds((c * FACES + k) * 128, 128), :]) for k in range(FACES)]
            highs = jnp.concatenate([block[0] for block in blocks], axis=1)
            lows = jnp.concatenate([block[1] for block in blocks], axis=1)
            high, low = left[x, y]
            stack = jnp.concatenate([high, low], axis=0)
            both = dot(
                jnp.concatenate([stack, stack], axis=1), jnp.concatenate([highs, lows], axis=0)
            )
            for k in range(FACES):
                tile = both[:, k * 128 : (k + 1) * 128]
                tile = jnp.where(low_lanes, tile[0:64] + tile[128:192], tile[64:128] + tile[192:256])
                yv[k, x, y * 64 : y * 64 + 64, :] = tile + pltpu.roll(tile, 64, 1)
    learn(1, False)

    copied(agg_v, 2).wait()
    copied(own_v, 3).wait()
    agg_rows = agg_v[...].reshape(4 * 2 * ny, 4 * nz).astype(F32).astype(BF16)
    shape = (16, 4 * 2 * ny)
    line = iota(shape, 0)
    take = iota(shape, 1) == (line >> 2) * (2 * ny) + gy * 2 - 1 + (line & 3)
    near = dot(take.astype(BF16), agg_rows).astype(BF16)
    shape = (4 * nz, 384)
    lane = iota(shape, 1)
    take = iota(shape, 0) == gz * 4 + ((lane >> 3) & 3) + (lane >> 7) - 1
    near = dot(near, take.astype(BF16))
    lane = iota((1, 128), 1)
    element, z_at, y_high = (lane >> 3) & 7, (lane >> 3) & 3, ((lane >> 5) & 1) == 1

    def slot(x, dx, dy, dz):
        lanes = slice((dz + 1) * 128, (dz + 2) * 128)
        row = (x + 1 + dx) * 4 + 1 + dy
        return jnp.where(y_high, near[row + 1 : row + 2, lanes], near[row : row + 1, lanes])

    slots = [[slot(x, *step) for step in STEPS] for x in range(2)]
    owners = own_v[0].astype(F32)
    owner = [jnp.zeros((1, 128), F32)] * 2
    for s in range(AGGS):
        value = jnp.broadcast_to(owners[:, s : s + 1], (1, 128))
        owner = [jnp.where(slots[x][0] == s, value, owner[x]) for x in range(2)]
    place = [jnp.zeros((1, 128), F32)] * 2
    for m in range(AGGS):
        turn = [pltpu.roll(owner[x], 8 * m, 1) if m else owner[x] for x in range(2)]
        if m:
            for x in range(2):
                place[x] += jnp.where((turn[x] == owner[x]) & (element >= m), 1.0, 0.0)
        place[1] += jnp.where(turn[0] == owner[1], 1.0, 0.0)
    code = [owner[x] * 8.0 + place[x] for x in range(2)]

    row64 = iota((64, 128), 0).astype(F32)

    def selection(codes):
        return (row64 == codes).astype(BF16)

    fold = ((iota((256, 128), 0) & 15) == (iota((256, 128), 1) & 15)).astype(BF16)
    group = iota((16, 128), 1) >> 4

    def picked(block, partners):
        return [
            jnp.where(group == partner, block[i * 16 : i * 16 + 16], 0.0)
            for i, partner in enumerate(partners)
        ]

    def flat(parts):
        count = len(parts)
        tall = dot(jnp.concatenate(split(jnp.concatenate(parts, axis=0)), axis=1), fold)
        tall = tall.reshape(count * 2, 8, 128)
        on_c = iota((count * 2, 8, 128), 1) == (iota((count * 2, 8, 128), 2) >> 4)
        tall = jnp.where(on_c, tall, 0.0).reshape(count, 2, 8, 128)
        return [jnp.concatenate([tall[i, 0], tall[i, 1]], axis=1) for i in range(count)]

    def summed(codes, rows):
        factors = []
        for i in range(len(codes)):
            factors += split(jnp.concatenate(rows[i * 8 : i * 8 + 8], axis=0))
        return dot(
            jnp.concatenate([selection(code) for code in codes], axis=1),
            jnp.concatenate(factors, axis=0),
        )

    def wide(value):
        return jnp.concatenate(split(value), axis=1)

    own = tuple(range(8))
    z_odd = (z_at & 1) == 1
    none = jnp.zeros((8, 256), F32)
    parts, codes = [], []
    for x in range(2):
        y = [yv[k, x] for k in range(FACES)]
        at = [[y[k][e * 16 : e * 16 + 16] for e in range(8)] for k in (5, 6)]
        lhs = (
            [y[0], yv[1 + x, 1 - x], y[4][:64], y[3][64:]]
            + [at[1 - (e & 1)][e] for e in own]
            + [at[e & 1][e] for e in (1, 2, 5, 6)]
        )
        partners = (
            own + own + tuple(e ^ 4 for e in own) + tuple(e ^ 1 for e in own) + (2, 1, 6, 5)
        )
        parts += picked(dot(wide(jnp.concatenate(lhs, axis=0)), own_rhs[x]), partners)
        other = 1 - x
        codes += [
            owner[x] * 8.0 + slots[x][0],
            owner[other] * 8.0 + slots[other][2 - other],
            owner[x] * 8.0 + jnp.where(y_high, slots[x][3], slots[x][4]),
            owner[x] * 8.0 + jnp.where(z_odd, slots[x][5], slots[x][6]),
            owner[x] * 8.0
            + jnp.where(z_at == 1, slots[x][6], jnp.where(z_at == 2, slots[x][5], -1000.0)),
        ]
    rows = flat(parts)
    padded = []
    for x in range(2):
        part = rows[x * 36 : x * 36 + 36]
        padded += part[:32] + [none, part[32], part[33], none, none, part[34], part[35], none]
    inner_rows = summed(codes, padded)

    def put(at, rows):
        for o in range(AGGS):
            for h in range(rows.shape[1] // 128):
                msg[pl.ds(o * 48 + at + h * 8, 8), :] = rows[
                    o * 8 : o * 8 + 8, h * 128 : (h + 1) * 128
                ]

    def rows_of(device_at, at, count):
        return pl.ds(pl.multiple_of(device_at * 48 + at, 16), count)

    def send(d, at, count):
        target = device(0, 0, d)
        pltpu.make_async_remote_copy(
            src_ref=msg.at[rows_of(target[2], at, count)],
            dst_ref=recv.at[rows_of(gz, at, count)],
            send_sem=row_send.at[0], recv_sem=row_recv.at[0],
            device_id=target, device_id_type=MESH,
        ).start()

    later = {d: late(1 if d > 0 else -1, abs(d)) for d in (2, -2, 3, -3)}
    later[4] = jnp.where(gz < nz // 2, late(1, 4), late(-1, 4))

    def send_all(at, count):
        for d in (1, -1):
            send(d, at, count)
        for d in later:
            pl.when(~later[d])(functools.partial(send, d, at, count))

    put(0, inner_rows)
    learn(2, False)
    send_all(0, 16)

    def when(flag, value, other):
        return jnp.where(jnp.full((1, 128), flag), value, other)

    label = [
        [
            when(inside[0], slots[0][1] + 1.0, 0.0),
            when(inside[1], slots[1][2] + 9.0, 0.0),
        ],
        [
            jnp.where(
                y_high,
                when(inside[3], slots[x][4] + 9.0, 0.0),
                when(inside[2], slots[x][3] + 1.0, 0.0),
            )
            for x in range(2)
        ],
        [
            jnp.where(
                z_at == 0,
                when(inside[4], slots[x][5] + 1.0, 0.0),
                jnp.where(z_at == 3, when(inside[5], slots[x][6] + 9.0, 0.0), 0.0),
            )
            for x in range(2)
        ],
    ]
    row, lane_all = iota((128, 128), 0), iota((128, 128), 1)
    once = ((lane_all & 7) == 0) & (lane_all < 64)
    which, who = [], []
    for x in range(2):
        value = jnp.where(
            row < 4, label[0][x], jnp.where(row < 8, label[1][x], jnp.where(row < 12, label[2][x], 0.0))
        )
        value = jnp.where(once & ((row & 3).astype(F32) == place[x]), value, 0.0)
        which.append(value.astype(BF16))
        who.append((iota((8, 128), 0).astype(F32) == owner[x]).astype(BF16))
    labels = lax.dot_general(
        jnp.concatenate(who, axis=1), jnp.concatenate(which, axis=1),
        (((1,), (1,)), ((), ())), preferred_element_type=F32,
    )

    edge_codes = [
        code[0],
        code[1],
        jnp.where(y_high, pltpu.roll(code[1], 32, 1), code[0]) + 4.0,
        jnp.where(y_high, code[1], pltpu.roll(code[0], 96, 1)) + 4.0,
    ]
    edge_codes = [when(inside[i], edge_codes[i], -1.0) for i in range(4)]
    z_code = jnp.full((1, 128), -1.0, F32)
    for side in range(2):
        for x in range(2):
            for y in range(2):
                to, at = side * 4 + x * 2 + y, y * 4 + side * 3
                turn = (8 * (to - at)) % 128
                value = pltpu.roll(code[x], turn, 1) if turn else code[x]
                z_code = jnp.where(element == to, when(inside[4 + side], value, -1.0), z_code)

    for face in range(6):
        pl.when(inside[face])(functools.partial(halo_wait, face))

    def halo_rhs(i):
        return stacked(columns_of(slabs[i]))

    def rows_y(k, y):
        return jnp.concatenate([yv[k, x, y * 64 : y * 64 + 64] for x in range(2)], axis=0)

    def rows_z(k, z):
        return [
            yv[k, x, y * 64 + z * 16 : y * 64 + z * 16 + 16] for x in range(2) for y in range(2)
        ]

    ends = jnp.concatenate(rows_z(5, 0) + rows_z(6, 3), axis=0)
    sides = [yv[1, 0], yv[2, 1], rows_y(3, 0), rows_y(4, 1), ends]
    parts = []
    for i in range(5):
        parts += picked(dot(wide(sides[i]), halo_rhs(2 + i)), own)
    rows = flat(parts)
    put(16, summed(edge_codes, rows[:32]))
    edges = summed([z_code], rows[32:])
    put(32, edges[:, :128] + pltpu.roll(edges[:, 128:], 4, 0))
    for o in range(AGGS):
        msg[pl.ds(o * 48 + 40, 1), :] = labels[o : o + 1]

    send_all(16, 25)
    stay = pltpu.make_async_copy(
        msg.at[rows_of(gz, 0, 41)], recv.at[rows_of(gz, 0, 41)], local_sem.at[0]
    )
    stay.start()
    for stage in range(3):
        learn(stage, True)
        for d in (stage + 2, -stage - 2) if stage < 2 else (4,):
            pl.when(later[d])(functools.partial(send, d, 0, 41))

    others = pltpu.make_async_remote_copy(
        src_ref=msg.at[pl.ds(0, 287)], dst_ref=recv.at[pl.ds(0, 287)],
        send_sem=row_send.at[0], recv_sem=row_recv.at[0],
        device_id=device(0, 0, 1), device_id_type=MESH,
    )
    others.wait_send()
    others.wait_recv()
    stay.wait()


def spread(recv, out_ref):
    def came(row):
        return recv[pl.ds(row, 8, stride=48), :]

    for s in range(AGGS):
        for h in range(2):
            out_ref[:, s * 256 + h * 128 : s * 256 + h * 128 + 128] = came(h * 8 + s)
    marks = came(40)
    for axis in range(3):
        first, step = (16 + axis * 4, 8) if axis < 2 else (32, 4)
        values = [[came(first + h * step + p) for h in range(2)] for p in range(4)]
        tags = [
            jnp.broadcast_to(marks[:, axis * 4 + p : axis * 4 + p + 1], (8, 128)) for p in range(4)
        ]
        for column in range(16):
            hits = [tag == column + 1.0 for tag in tags]
            for h in range(2):
                total = jnp.where(hits[0], values[0][h], 0.0)
                for p in range(1, 4):
                    total += jnp.where(hits[p], values[p][h], 0.0)
                at_lane = (AGGS * (1 + 2 * axis) + column) * 256 + h * 128
                out_ref[:, at_lane : at_lane + 128] = total


def solution(mesh):
    sizes = (mesh.shape["gx"], mesh.shape["gy"], mesh.shape["gz"])

    def shards(fine_blocks, prolong, agg_map, owner_map):
        fine = fine_blocks.transpose(0, 1, 3, 2, 4).reshape(2, 2, 7, 4, 32, 128)
        fine = fine.transpose(0, 1, 2, 4, 3, 5).reshape(3584, 128)
        base = prolong.reshape(2, 2, 4, 8, 128).transpose(0, 1, 3, 2, 4)
        fine, base, agg_map, owner_map = (
            pltpu.with_memory_space_constraint(value, pltpu.HBM)
            for value in (fine, base, agg_map, owner_map)
        )
        rows = pl.pallas_call(
            functools.partial(kernel, sizes),
            out_shape=jax.ShapeDtypeStruct((384, 128), F32),
            in_specs=[pl.BlockSpec(memory_space=pltpu.HBM)] * 4,
            out_specs=pl.BlockSpec(memory_space=pltpu.VMEM),
            scratch_shapes=[
                pltpu.VMEM((3584, 128), F32),
                pltpu.VMEM((7, 8, 8, 128), F32),
                pltpu.VMEM((4,) + agg_map.shape[1:], jnp.int32),
                pltpu.VMEM((1, 1, AGGS), jnp.int32),
                pltpu.VMEM((FACES, 2, 128, 128), F32),
                pltpu.VMEM((384, 128), F32),
                pltpu.SemaphoreType.DMA((4,)),
                pltpu.SemaphoreType.DMA((6,)),
                pltpu.SemaphoreType.DMA((6,)),
                pltpu.SemaphoreType.DMA((1,)),
                pltpu.SemaphoreType.DMA((1,)),
                pltpu.SemaphoreType.REGULAR((2, 3)),
            ],
            compiler_params=pltpu.CompilerParams(
                collective_id=0, has_side_effects=True, vmem_limit_bytes=16 << 20
            ),
        )(fine, base, agg_map, owner_map)
        result = pl.pallas_call(
            spread,
            out_shape=jax.ShapeDtypeStruct((AGGS, 7 * AGGS * 256), F32),
            in_specs=[pl.BlockSpec(memory_space=pltpu.VMEM)],
            out_specs=pl.BlockSpec(memory_space=pltpu.VMEM),
            compiler_params=pltpu.CompilerParams(vmem_limit_bytes=8 << 20),
        )(rows)
        return result.reshape(1, 1, AGGS, 7 * AGGS * 256)

    placed = (P("gx", "gy", "gz", None, None), P("gx", "gy", "gz", None), P(), P("gx", "gy", "gz"))
    return jax.shard_map(
        shards, mesh=mesh, in_specs=placed, out_specs=P("gx", "gy", "gz", None), check_vma=False
    )
```

```python
import functools

import jax
import jax.numpy as jnp
from jax import lax
from jax.experimental import pallas as pl
from jax.experimental.pallas import tpu as pltpu
from jax.sharding import PartitionSpec as P

MESH = pl.DeviceIdType.MESH
F32 = jnp.float32
BF16 = jnp.bfloat16
AGGS = 8
FACES = 7
STEPS = ((0, 0, 0), (-1, 0, 0), (1, 0, 0), (0, -1, 0), (0, 1, 0), (0, 0, -1), (0, 0, 1))


def iota(shape, dim):
    return lax.broadcasted_iota(jnp.int32, shape, dim)


def split(value):
    high = value.astype(BF16)
    return high, (value - high.astype(F32)).astype(BF16)


def dot(a, b):
    return jnp.dot(a, b, preferred_element_type=F32)


def columns_of(slab):
    row, group = iota((8, 8, 128), 1), iota((8, 8, 128), 2) >> 4
    for bit in (4, 2, 1):
        row_bit, group_bit = row & bit, group & bit
        down = pltpu.roll(pltpu.roll(slab, 128 - 16 * bit, 2), bit, 1)
        if bit == 4:
            slab = jnp.where(row_bit == group_bit, slab, down)
        else:
            up = pltpu.roll(pltpu.roll(slab, 16 * bit, 2), 8 - bit, 1)
            slab = jnp.where(row_bit == group_bit, slab, jnp.where(row_bit > 0, down, up))
    return slab.reshape(64, 128)


def stacked(cols):
    high, low = split(cols)
    return jnp.concatenate([high, low, high, low], axis=0)


def kernel(
    sizes, a_hbm, p_hbm, agg_hbm, own_hbm, recv,
    a_v, slabs, faces, sides_in, agg_v, own_v, yv, msg,
    local_sem, halo_send, halo_recv, row_send, row_recv, ready,
):
    nx, ny, nz = sizes
    gx, gy, gz = lax.axis_index("gx"), lax.axis_index("gy"), lax.axis_index("gz")

    def device(dx, dy, dz):
        return (
            lax.rem(gx + dx + nx, nx),
            lax.rem(gy + dy + ny, ny),
            lax.rem(gz + dz + nz, nz),
        )

    def signal(sem, target):
        pl.semaphore_signal(sem, inc=1, device_id=target, device_id_type=MESH)

    inside = (gx > 0, gx < nx - 1, gy > 0, gy < ny - 1, gz > 0, gz < nz - 1)

    def copied(dst, n):
        return pltpu.make_async_copy(dst, dst, local_sem.at[n])

    for x in range(2):
        for y in range(2):
            half = pl.ds(4 * y, 4)
            pltpu.make_async_copy(
                p_hbm.at[x, y], slabs.at[x, :, half, :], local_sem.at[0]
            ).start()
    for c in range(4):
        rows = pl.ds(c * 896, 896)
        pltpu.make_async_copy(a_hbm.at[rows], a_v.at[rows], local_sem.at[1]).start()
    for plane in range(4):
        where = jnp.clip(gx * 2 - 1 + plane, 0, 2 * nx - 1)
        pltpu.make_async_copy(
            agg_hbm.at[pl.ds(where, 1)], agg_v.at[pl.ds(plane, 1)], local_sem.at[2]
        ).start()
    pltpu.make_async_copy(own_hbm, own_v, local_sem.at[3]).start()

    barrier = pltpu.get_barrier_semaphore()
    for n, step in enumerate(STEPS[1:]):
        if n < 4:
            pl.when(inside[n])(functools.partial(signal, barrier, device(*step)))
        else:
            signal(barrier, device(*step))

    halo = [[] for _ in range(6)]

    def halo_copy(face, src, dst):
        halo[face].append(
            pltpu.make_async_remote_copy(
                src_ref=src, dst_ref=dst,
                send_sem=halo_send.at[face], recv_sem=halo_recv.at[face],
                device_id=device(*STEPS[1 + face]), device_id_type=MESH,
            )
        )

    for face in range(4):
        halo_copy(face, faces.at[face], sides_in.at[face ^ 1])
    for u in range(2):
        for v in range(2):
            halo_copy(4, p_hbm.at[u, v, :, 0, :], slabs.at[2, :, 4 + u * 2 + v, :])
            halo_copy(5, p_hbm.at[u, v, :, 3, :], slabs.at[2, :, u * 2 + v, :])

    def halo_wait(face):
        slab = sides_in.at[face] if face < 4 else slabs.at[2, :, pl.ds((face - 4) * 4, 4), :]
        done = pltpu.make_async_remote_copy(
            src_ref=slab, dst_ref=slab,
            send_sem=halo_send.at[face], recv_sem=halo_recv.at[face ^ 1],
            device_id=device(*STEPS[1 + face]), device_id_type=MESH,
        )
        done.wait_send()
        done.wait_recv()

    past = {1: lax.rem(nz - gz, nz), -1: gz}
    ways = ((0, 1), (1, -1))

    def late(way, d):
        return (past[way] >= 1) & (past[way] <= d)

    def learn(stage, last):
        for n, way in ways:
            flag = late(way, stage + 2)

            @pl.when(flag if last else ~flag)
            def _():
                pl.semaphore_wait(ready.at[n, stage], 1)
                if stage < 2:
                    signal(ready.at[n, stage + 1], device(0, 0, -way))

    def send_faces(which):
        for face in which:

            @pl.when(inside[face])
            def _():
                for copy in halo[face]:
                    copy.start()

    def meet():
        pl.semaphore_wait(barrier, 2 + sum(flag.astype(jnp.int32) for flag in inside[:4]))
        send_faces((4, 5))

        for n, way in ways:
            signal(ready.at[n, 0], device(0, 0, -way))
        for face in range(4):

            @pl.when(~inside[face])
            def _():
                sides_in[face] = jnp.zeros((64, 128), F32)

        for face in (4, 5):

            @pl.when(~inside[face])
            def _():
                slabs[2, :, (face - 4) * 4 : (face - 4) * 4 + 4, :] = jnp.zeros((8, 4, 128), F32)

    meet()

    copied(slabs.at[pl.ds(0, 2)], 0).wait()
    own_cols = [columns_of(slabs[x]) for x in range(2)]
    own_rhs = [stacked(cols) for cols in own_cols]
    low_lanes = iota((64, 128), 1) < 64
    for x in range(2):
        faces[x] = own_cols[x]
    faces[2] = jnp.where(low_lanes, own_cols[0], pltpu.roll(own_cols[1], 64, 1))
    faces[3] = jnp.where(low_lanes, pltpu.roll(own_cols[0], 64, 1), own_cols[1])
    turned = jnp.concatenate(split(jnp.concatenate(own_cols, axis=0).T), axis=0)
    lane = iota((128, 256), 1)
    spot = 2 * ((lane & 127) >> 2) + (lane >> 7)
    keep = ((iota((256, 256), 0) >> 4) & 3) == (iota((256, 256), 1) & 3)
    left = {}
    for x in range(2):
        spread = (iota((128, 256), 0) == spot + 64 * x).astype(BF16)
        wide = jnp.where(keep, dot(turned, spread), 0.0).astype(BF16)
        for y in range(2):
            parts = []
            for at in (y * 64, 128 + y * 64):
                rows = wide[at : at + 64]
                parts.append(jnp.concatenate([rows[:, :128], rows[:, 128:]], axis=0))
            left[x, y] = parts

    send_faces((2, 3, 0, 1))

    learn(0, False)
    copied(a_v, 1).wait()
    for x in range(2):
        for y in range(2):
            c = x * 2 + y
            blocks = [split(a_v[pl.ds((c * FACES + k) * 128, 128), :]) for k in range(FACES)]
            highs = jnp.concatenate([block[0] for block in blocks], axis=1)
            lows = jnp.concatenate([block[1] for block in blocks], axis=1)
            high, low = left[x, y]
            stack = jnp.concatenate([high, low], axis=0)
            both = dot(
                jnp.concatenate([stack, stack], axis=1), jnp.concatenate([highs, lows], axis=0)
            )
            for k in range(FACES):
                tile = both[:, k * 128 : (k + 1) * 128]
                tile = jnp.where(low_lanes, tile[0:64] + tile[128:192], tile[64:128] + tile[192:256])
                yv[k, x, y * 64 : y * 64 + 64, :] = tile + pltpu.roll(tile, 64, 1)
    learn(1, False)

    copied(agg_v, 2).wait()
    copied(own_v, 3).wait()
    agg_rows = agg_v[...].reshape(4 * 2 * ny, 4 * nz).astype(F32).astype(BF16)
    shape = (16, 4 * 2 * ny)
    line = iota(shape, 0)
    take = iota(shape, 1) == (line >> 2) * (2 * ny) + gy * 2 - 1 + (line & 3)
    near = dot(take.astype(BF16), agg_rows).astype(BF16)
    shape = (4 * nz, 384)
    lane = iota(shape, 1)
    take = iota(shape, 0) == gz * 4 + ((lane >> 3) & 3) + (lane >> 7) - 1
    near = dot(near, take.astype(BF16))
    lane = iota((1, 128), 1)
    element, z_at, y_high = (lane >> 3) & 7, (lane >> 3) & 3, ((lane >> 5) & 1) == 1

    def slot(x, dx, dy, dz):
        lanes = slice((dz + 1) * 128, (dz + 2) * 128)
        row = (x + 1 + dx) * 4 + 1 + dy
        return jnp.where(y_high, near[row + 1 : row + 2, lanes], near[row : row + 1, lanes])

    slots = [[slot(x, *step) for step in STEPS] for x in range(2)]
    owners = own_v[0].astype(F32)
    owner = [jnp.zeros((1, 128), F32)] * 2
    for s in range(AGGS):
        value = jnp.broadcast_to(owners[:, s : s + 1], (1, 128))
        owner = [jnp.where(slots[x][0] == s, value, owner[x]) for x in range(2)]
    place = [jnp.zeros((1, 128), F32)] * 2
    for m in range(AGGS):
        turn = [pltpu.roll(owner[x], 8 * m, 1) if m else owner[x] for x in range(2)]
        if m:
            for x in range(2):
                place[x] += jnp.where((turn[x] == owner[x]) & (element >= m), 1.0, 0.0)
        place[1] += jnp.where(turn[0] == owner[1], 1.0, 0.0)
    code = [owner[x] * 8.0 + place[x] for x in range(2)]

    row64 = iota((64, 128), 0).astype(F32)

    def selection(codes):
        return (row64 == codes).astype(BF16)

    fold = ((iota((256, 128), 0) & 15) == (iota((256, 128), 1) & 15)).astype(BF16)
    group = iota((16, 128), 1) >> 4

    def picked(block, partners):
        return [
            jnp.where(group == partner, block[i * 16 : i * 16 + 16], 0.0)
            for i, partner in enumerate(partners)
        ]

    def flat(parts):
        count = len(parts)
        tall = dot(jnp.concatenate(split(jnp.concatenate(parts, axis=0)), axis=1), fold)
        tall = tall.reshape(count * 2, 8, 128)
        on_c = iota((count * 2, 8, 128), 1) == (iota((count * 2, 8, 128), 2) >> 4)
        tall = jnp.where(on_c, tall, 0.0).reshape(count, 2, 8, 128)
        return [jnp.concatenate([tall[i, 0], tall[i, 1]], axis=1) for i in range(count)]

    def summed(codes, rows):
        factors = []
        for i in range(len(codes)):
            factors += split(jnp.concatenate(rows[i * 8 : i * 8 + 8], axis=0))
        return dot(
            jnp.concatenate([selection(code) for code in codes], axis=1),
            jnp.concatenate(factors, axis=0),
        )

    def wide(value):
        return jnp.concatenate(split(value), axis=1)

    own = tuple(range(8))
    z_odd = (z_at & 1) == 1
    none = jnp.zeros((8, 256), F32)
    parts, codes = [], []
    for x in range(2):
        y = [yv[k, x] for k in range(FACES)]
        at = [[y[k][e * 16 : e * 16 + 16] for e in range(8)] for k in (5, 6)]
        lhs = (
            [y[0], yv[1 + x, 1 - x], y[4][:64], y[3][64:]]
            + [at[1 - (e & 1)][e] for e in own]
            + [at[e & 1][e] for e in (1, 2, 5, 6)]
        )
        partners = (
            own + own + tuple(e ^ 4 for e in own) + tuple(e ^ 1 for e in own) + (2, 1, 6, 5)
        )
        parts += picked(dot(wide(jnp.concatenate(lhs, axis=0)), own_rhs[x]), partners)
        other = 1 - x
        codes += [
            owner[x] * 8.0 + slots[x][0],
            owner[other] * 8.0 + slots[other][2 - other],
            owner[x] * 8.0 + jnp.where(y_high, slots[x][3], slots[x][4]),
            owner[x] * 8.0 + jnp.where(z_odd, slots[x][5], slots[x][6]),
            owner[x] * 8.0
            + jnp.where(z_at == 1, slots[x][6], jnp.where(z_at == 2, slots[x][5], -1000.0)),
        ]
    rows = flat(parts)
    padded = []
    for x in range(2):
        part = rows[x * 36 : x * 36 + 36]
        padded += part[:32] + [none, part[32], part[33], none, none, part[34], part[35], none]
    inner_rows = summed(codes, padded)

    def put(at, rows):
        for o in range(AGGS):
            for h in range(rows.shape[1] // 128):
                msg[pl.ds(o * 48 + at + h * 8, 8), :] = rows[
                    o * 8 : o * 8 + 8, h * 128 : (h + 1) * 128
                ]

    def rows_of(device_at, at, count):
        return pl.ds(pl.multiple_of(device_at * 48 + at, 16), count)

    def send(d, at, count):
        target = device(0, 0, d)
        pltpu.make_async_remote_copy(
            src_ref=msg.at[rows_of(target[2], at, count)],
            dst_ref=recv.at[rows_of(gz, at, count)],
            send_sem=row_send.at[0], recv_sem=row_recv.at[0],
            device_id=target, device_id_type=MESH,
        ).start()

    later = {d: late(1 if d > 0 else -1, abs(d)) for d in (2, -2, 3, -3)}
    later[4] = jnp.where(gz < nz // 2, late(1, 4), late(-1, 4))

    def send_all(at, count):
        for d in (1, -1):
            send(d, at, count)
        for d in later:
            pl.when(~later[d])(functools.partial(send, d, at, count))

    put(0, inner_rows)
    learn(2, False)
    send_all(0, 16)

    def when(flag, value, other):
        return jnp.where(jnp.full((1, 128), flag), value, other)

    label = [
        [
            when(inside[0], slots[0][1] + 1.0, 0.0),
            when(inside[1], slots[1][2] + 9.0, 0.0),
        ],
        [
            jnp.where(
                y_high,
                when(inside[3], slots[x][4] + 9.0, 0.0),
                when(inside[2], slots[x][3] + 1.0, 0.0),
            )
            for x in range(2)
        ],
        [
            jnp.where(
                z_at == 0,
                when(inside[4], slots[x][5] + 1.0, 0.0),
                jnp.where(z_at == 3, when(inside[5], slots[x][6] + 9.0, 0.0), 0.0),
            )
            for x in range(2)
        ],
    ]
    row, lane_all = iota((128, 128), 0), iota((128, 128), 1)
    once = ((lane_all & 7) == 0) & (lane_all < 64)
    which, who = [], []
    for x in range(2):
        value = jnp.where(
            row < 4, label[0][x], jnp.where(row < 8, label[1][x], jnp.where(row < 12, label[2][x], 0.0))
        )
        value = jnp.where(once & ((row & 3).astype(F32) == place[x]), value, 0.0)
        which.append(value.astype(BF16))
        who.append((iota((8, 128), 0).astype(F32) == owner[x]).astype(BF16))
    labels = lax.dot_general(
        jnp.concatenate(who, axis=1), jnp.concatenate(which, axis=1),
        (((1,), (1,)), ((), ())), preferred_element_type=F32,
    )

    edge_codes = [
        code[0],
        code[1],
        jnp.where(y_high, pltpu.roll(code[1], 32, 1), code[0]) + 4.0,
        jnp.where(y_high, code[1], pltpu.roll(code[0], 96, 1)) + 4.0,
    ]
    edge_codes = [when(inside[i], edge_codes[i], -1.0) for i in range(4)]
    z_code = jnp.full((1, 128), -1.0, F32)
    for side in range(2):
        for x in range(2):
            for y in range(2):
                to, at = side * 4 + x * 2 + y, y * 4 + side * 3
                turn = (8 * (to - at)) % 128
                value = pltpu.roll(code[x], turn, 1) if turn else code[x]
                z_code = jnp.where(element == to, when(inside[4 + side], value, -1.0), z_code)

    for face in range(6):
        pl.when(inside[face])(functools.partial(halo_wait, face))

    def halo_rhs(face):
        return stacked(sides_in[face] if face < 4 else columns_of(slabs[2]))

    def rows_y(k, y):
        return jnp.concatenate([yv[k, x, y * 64 : y * 64 + 64] for x in range(2)], axis=0)

    def rows_z(k, z):
        return [
            yv[k, x, y * 64 + z * 16 : y * 64 + z * 16 + 16] for x in range(2) for y in range(2)
        ]

    ends = jnp.concatenate(rows_z(5, 0) + rows_z(6, 3), axis=0)
    sides = [yv[1, 0], yv[2, 1], rows_y(3, 0), rows_y(4, 1), ends]
    parts = []
    for i in range(5):
        parts += picked(dot(wide(sides[i]), halo_rhs(i)), own)
    rows = flat(parts)
    put(16, summed(edge_codes, rows[:32]))
    edges = summed([z_code], rows[32:])
    put(32, edges[:, :128] + pltpu.roll(edges[:, 128:], 4, 0))
    for o in range(AGGS):
        msg[pl.ds(o * 48 + 40, 1), :] = labels[o : o + 1]

    send_all(16, 25)
    stay = pltpu.make_async_copy(
        msg.at[rows_of(gz, 0, 41)], recv.at[rows_of(gz, 0, 41)], local_sem.at[0]
    )
    stay.start()
    for stage in range(3):
        learn(stage, True)
        for d in (stage + 2, -stage - 2) if stage < 2 else (4,):
            pl.when(later[d])(functools.partial(send, d, 0, 41))

    others = pltpu.make_async_remote_copy(
        src_ref=msg.at[pl.ds(0, 287)], dst_ref=recv.at[pl.ds(0, 287)],
        send_sem=row_send.at[0], recv_sem=row_recv.at[0],
        device_id=device(0, 0, 1), device_id_type=MESH,
    )
    others.wait_send()
    others.wait_recv()
    stay.wait()


def spread(recv, out_hbm, out_ref, sem):
    pieces = []

    def write(start, lanes):
        piece = (slice(None), pl.ds(start, lanes))
        pieces.append(
            pltpu.make_async_copy(out_ref.at[piece], out_hbm.at[piece], sem.at[len(pieces)])
        )
        pieces[-1].start()

    def came(row):
        return recv[pl.ds(row, 8, stride=48), :]

    for s in range(AGGS):
        for h in range(2):
            out_ref[:, s * 256 + h * 128 : s * 256 + h * 128 + 128] = came(h * 8 + s)
    write(0, AGGS * 256)
    marks = came(40)
    for axis in range(3):
        first, step = (16 + axis * 4, 8) if axis < 2 else (32, 4)
        values = [[came(first + h * step + p) for h in range(2)] for p in range(4)]
        tags = [
            jnp.broadcast_to(marks[:, axis * 4 + p : axis * 4 + p + 1], (8, 128)) for p in range(4)
        ]
        for column in range(16):
            hits = [tag == column + 1.0 for tag in tags]
            for h in range(2):
                total = jnp.where(hits[0], values[0][h], 0.0)
                for p in range(1, 4):
                    total += jnp.where(hits[p], values[p][h], 0.0)
                at_lane = (AGGS * (1 + 2 * axis) + column) * 256 + h * 128
                out_ref[:, at_lane : at_lane + 128] = total
        write(AGGS * (1 + 2 * axis) * 256, AGGS * 512)
    for piece in pieces:
        piece.wait()


def solution(mesh):
    sizes = (mesh.shape["gx"], mesh.shape["gy"], mesh.shape["gz"])

    def shards(fine_blocks, prolong, agg_map, owner_map):
        fine = fine_blocks.transpose(0, 1, 3, 2, 4).reshape(2, 2, 7, 4, 32, 128)
        fine = fine.transpose(0, 1, 2, 4, 3, 5).reshape(3584, 128)
        base = prolong.reshape(2, 2, 4, 8, 128).transpose(0, 1, 3, 2, 4)
        fine, base, agg_map, owner_map = (
            pltpu.with_memory_space_constraint(value, pltpu.HBM)
            for value in (fine, base, agg_map, owner_map)
        )
        rows = pl.pallas_call(
            functools.partial(kernel, sizes),
            out_shape=jax.ShapeDtypeStruct((384, 128), F32),
            in_specs=[pl.BlockSpec(memory_space=pltpu.HBM)] * 4,
            out_specs=pl.BlockSpec(memory_space=pltpu.VMEM),
            scratch_shapes=[
                pltpu.VMEM((3584, 128), F32),
                pltpu.VMEM((3, 8, 8, 128), F32),
                pltpu.VMEM((4, 64, 128), F32),
                pltpu.VMEM((4, 64, 128), F32),
                pltpu.VMEM((4,) + agg_map.shape[1:], jnp.int32),
                pltpu.VMEM((1, 1, AGGS), jnp.int32),
                pltpu.VMEM((FACES, 2, 128, 128), F32),
                pltpu.VMEM((384, 128), F32),
                pltpu.SemaphoreType.DMA((4,)),
                pltpu.SemaphoreType.DMA((6,)),
                pltpu.SemaphoreType.DMA((6,)),
                pltpu.SemaphoreType.DMA((1,)),
                pltpu.SemaphoreType.DMA((1,)),
                pltpu.SemaphoreType.REGULAR((2, 3)),
            ],
            compiler_params=pltpu.CompilerParams(
                collective_id=0, has_side_effects=True, vmem_limit_bytes=16 << 20
            ),
        )(fine, base, agg_map, owner_map)
        result = pl.pallas_call(
            spread,
            out_shape=jax.ShapeDtypeStruct((AGGS, 7 * AGGS * 256), F32),
            in_specs=[pl.BlockSpec(memory_space=pltpu.VMEM)],
            out_specs=pl.BlockSpec(memory_space=pltpu.HBM),
            scratch_shapes=[
                pltpu.VMEM((AGGS, 7 * AGGS * 256), F32),
                pltpu.SemaphoreType.DMA((4,)),
            ],
            compiler_params=pltpu.CompilerParams(vmem_limit_bytes=8 << 20),
        )(rows)
        return result.reshape(1, 1, AGGS, 7 * AGGS * 256)

    placed = (P("gx", "gy", "gz", None, None), P("gx", "gy", "gz", None), P(), P("gx", "gy", "gz"))
    return jax.shard_map(
        shards, mesh=mesh, in_specs=placed, out_specs=P("gx", "gy", "gz", None), check_vma=False
    )
```

```python
import functools

import jax
import jax.numpy as jnp
from jax import lax
from jax.experimental import pallas as pl
from jax.experimental.pallas import tpu as pltpu
from jax.sharding import PartitionSpec as P

MESH = pl.DeviceIdType.MESH
F32 = jnp.float32
BF16 = jnp.bfloat16
AGGS = 8
FACES = 7
STEPS = ((0, 0, 0), (-1, 0, 0), (1, 0, 0), (0, -1, 0), (0, 1, 0), (0, 0, -1), (0, 0, 1))


def iota(shape, dim):
    return lax.broadcasted_iota(jnp.int32, shape, dim)


def split(value):
    high = value.astype(BF16)
    return high, (value - high.astype(F32)).astype(BF16)


def dot(a, b):
    return jnp.dot(a, b, preferred_element_type=F32)


def columns_of(slab):
    row, group = iota((8, 8, 128), 1), iota((8, 8, 128), 2) >> 4
    for bit in (4, 2, 1):
        row_bit, group_bit = row & bit, group & bit
        down = pltpu.roll(pltpu.roll(slab, 128 - 16 * bit, 2), bit, 1)
        if bit == 4:
            slab = jnp.where(row_bit == group_bit, slab, down)
        else:
            up = pltpu.roll(pltpu.roll(slab, 16 * bit, 2), 8 - bit, 1)
            slab = jnp.where(row_bit == group_bit, slab, jnp.where(row_bit > 0, down, up))
    return slab.reshape(64, 128)


def stacked(cols):
    high, low = split(cols)
    return jnp.concatenate([high, low, high, low], axis=0)


def kernel(
    sizes, a_hbm, p_hbm, agg_hbm, own_hbm, recv,
    a_v, slabs, faces, sides_in, agg_v, own_v, yv, msg,
    local_sem, halo_send, halo_recv, row_send, row_recv, ready,
):
    nx, ny, nz = sizes
    gx, gy, gz = lax.axis_index("gx"), lax.axis_index("gy"), lax.axis_index("gz")

    def device(dx, dy, dz):
        return (
            lax.rem(gx + dx + nx, nx),
            lax.rem(gy + dy + ny, ny),
            lax.rem(gz + dz + nz, nz),
        )

    def signal(sem, target):
        pl.semaphore_signal(sem, inc=1, device_id=target, device_id_type=MESH)

    inside = (gx > 0, gx < nx - 1, gy > 0, gy < ny - 1, gz > 0, gz < nz - 1)

    def copied(dst, n):
        return pltpu.make_async_copy(dst, dst, local_sem.at[n])

    for x in range(2):
        for y in range(2):
            half = pl.ds(4 * y, 4)
            pltpu.make_async_copy(
                p_hbm.at[x, y], slabs.at[x, :, half, :], local_sem.at[0]
            ).start()
    for c in range(4):
        rows = pl.ds(c * 896, 896)
        pltpu.make_async_copy(a_hbm.at[rows], a_v.at[rows], local_sem.at[1]).start()
    for plane in range(4):
        where = jnp.clip(gx * 2 - 1 + plane, 0, 2 * nx - 1)
        pltpu.make_async_copy(
            agg_hbm.at[pl.ds(where, 1)], agg_v.at[pl.ds(plane, 1)], local_sem.at[2]
        ).start()
    pltpu.make_async_copy(own_hbm, own_v, local_sem.at[3]).start()

    barrier = pltpu.get_barrier_semaphore()
    for n, step in enumerate(STEPS[1:]):
        if n < 4:
            pl.when(inside[n])(functools.partial(signal, barrier, device(*step)))
        else:
            signal(barrier, device(*step))

    halo = [[] for _ in range(6)]

    def halo_copy(face, src, dst):
        halo[face].append(
            pltpu.make_async_remote_copy(
                src_ref=src, dst_ref=dst,
                send_sem=halo_send.at[face], recv_sem=halo_recv.at[face],
                device_id=device(*STEPS[1 + face]), device_id_type=MESH,
            )
        )

    for face in range(4):
        halo_copy(face, faces.at[face], sides_in.at[face ^ 1])
    for u in range(2):
        for v in range(2):
            halo_copy(4, p_hbm.at[u, v, :, 0, :], slabs.at[2, :, 4 + u * 2 + v, :])
            halo_copy(5, p_hbm.at[u, v, :, 3, :], slabs.at[2, :, u * 2 + v, :])

    def halo_wait(face):
        slab = sides_in.at[face] if face < 4 else slabs.at[2, :, pl.ds((face - 4) * 4, 4), :]
        done = pltpu.make_async_remote_copy(
            src_ref=slab, dst_ref=slab,
            send_sem=halo_send.at[face], recv_sem=halo_recv.at[face ^ 1],
            device_id=device(*STEPS[1 + face]), device_id_type=MESH,
        )
        done.wait_send()
        done.wait_recv()

    past = {1: lax.rem(nz - gz, nz), -1: gz}
    ways = ((0, 1), (1, -1))

    def late(way, d):
        return (past[way] >= 1) & (past[way] <= d)

    def learn(stage, last):
        for n, way in ways:
            flag = late(way, stage + 2)

            @pl.when(flag if last else ~flag)
            def _():
                pl.semaphore_wait(ready.at[n, stage], 1)
                if stage < 2:
                    signal(ready.at[n, stage + 1], device(0, 0, -way))

    def send_faces(which):
        for face in which:

            @pl.when(inside[face])
            def _():
                for copy in halo[face]:
                    copy.start()

    def meet():
        pl.semaphore_wait(barrier, 2 + sum(flag.astype(jnp.int32) for flag in inside[:4]))
        send_faces((4, 5))

        for n, way in ways:
            signal(ready.at[n, 0], device(0, 0, -way))
        for face in range(4):

            @pl.when(~inside[face])
            def _():
                sides_in[face] = jnp.zeros((64, 128), F32)

        for face in (4, 5):

            @pl.when(~inside[face])
            def _():
                slabs[2, :, (face - 4) * 4 : (face - 4) * 4 + 4, :] = jnp.zeros((8, 4, 128), F32)

    meet()

    copied(slabs.at[pl.ds(0, 2)], 0).wait()
    own_cols = [columns_of(slabs[x]) for x in range(2)]
    own_rhs = [stacked(cols) for cols in own_cols]
    low_lanes = iota((64, 128), 1) < 64
    for x in range(2):
        faces[x] = own_cols[x]
    faces[2] = jnp.where(low_lanes, own_cols[0], pltpu.roll(own_cols[1], 64, 1))
    faces[3] = jnp.where(low_lanes, pltpu.roll(own_cols[0], 64, 1), own_cols[1])
    turned = jnp.concatenate(split(jnp.concatenate(own_cols, axis=0).T), axis=0)
    lane = iota((128, 256), 1)
    spot = 2 * ((lane & 127) >> 2) + (lane >> 7)
    keep = ((iota((256, 256), 0) >> 4) & 3) == (iota((256, 256), 1) & 3)
    left = {}
    for x in range(2):
        spread = (iota((128, 256), 0) == spot + 64 * x).astype(BF16)
        wide = jnp.where(keep, dot(turned, spread), 0.0).astype(BF16)
        for y in range(2):
            parts = []
            for at in (y * 64, 128 + y * 64):
                rows = wide[at : at + 64]
                parts.append(jnp.concatenate([rows[:, :128], rows[:, 128:]], axis=0))
            left[x, y] = parts

    send_faces((2, 3, 0, 1))

    learn(0, False)
    copied(a_v, 1).wait()
    for x in range(2):
        for y in range(2):
            c = x * 2 + y
            blocks = [split(a_v[pl.ds((c * FACES + k) * 128, 128), :]) for k in range(FACES)]
            highs = jnp.concatenate([block[0] for block in blocks], axis=1)
            lows = jnp.concatenate([block[1] for block in blocks], axis=1)
            high, low = left[x, y]
            stack = jnp.concatenate([high, low], axis=0)
            both = dot(
                jnp.concatenate([stack, stack], axis=1), jnp.concatenate([highs, lows], axis=0)
            )
            for k in range(FACES):
                tile = both[:, k * 128 : (k + 1) * 128]
                tile = jnp.where(low_lanes, tile[0:64] + tile[128:192], tile[64:128] + tile[192:256])
                yv[k, x, y * 64 : y * 64 + 64, :] = tile + pltpu.roll(tile, 64, 1)
    learn(1, False)

    copied(agg_v, 2).wait()
    copied(own_v, 3).wait()
    agg_rows = agg_v[...].reshape(4 * 2 * ny, 4 * nz).astype(F32).astype(BF16)
    shape = (16, 4 * 2 * ny)
    line = iota(shape, 0)
    take = iota(shape, 1) == (line >> 2) * (2 * ny) + gy * 2 - 1 + (line & 3)
    near = dot(take.astype(BF16), agg_rows).astype(BF16)
    shape = (4 * nz, 384)
    lane = iota(shape, 1)
    take = iota(shape, 0) == gz * 4 + ((lane >> 3) & 3) + (lane >> 7) - 1
    near = dot(near, take.astype(BF16))
    lane = iota((1, 128), 1)
    element, z_at, y_high = (lane >> 3) & 7, (lane >> 3) & 3, ((lane >> 5) & 1) == 1

    def slot(x, dx, dy, dz):
        lanes = slice((dz + 1) * 128, (dz + 2) * 128)
        row = (x + 1 + dx) * 4 + 1 + dy
        return jnp.where(y_high, near[row + 1 : row + 2, lanes], near[row : row + 1, lanes])

    slots = [[slot(x, *step) for step in STEPS] for x in range(2)]
    owners = own_v[0].astype(F32)
    owner = [jnp.zeros((1, 128), F32)] * 2
    for s in range(AGGS):
        value = jnp.broadcast_to(owners[:, s : s + 1], (1, 128))
        owner = [jnp.where(slots[x][0] == s, value, owner[x]) for x in range(2)]
    place = [jnp.zeros((1, 128), F32)] * 2
    for m in range(AGGS):
        turn = [pltpu.roll(owner[x], 8 * m, 1) if m else owner[x] for x in range(2)]
        if m:
            for x in range(2):
                place[x] += jnp.where((turn[x] == owner[x]) & (element >= m), 1.0, 0.0)
        place[1] += jnp.where(turn[0] == owner[1], 1.0, 0.0)
    code = [owner[x] * 8.0 + place[x] for x in range(2)]

    row64 = iota((64, 128), 0).astype(F32)

    def selection(codes):
        return (row64 == codes).astype(BF16)

    fold = ((iota((256, 128), 0) & 15) == (iota((256, 128), 1) & 15)).astype(BF16)
    group = iota((16, 128), 1) >> 4

    def picked(block, partners):
        return [
            jnp.where(group == partner, block[i * 16 : i * 16 + 16], 0.0)
            for i, partner in enumerate(partners)
        ]

    def flat(parts):
        count = len(parts)
        tall = dot(jnp.concatenate(split(jnp.concatenate(parts, axis=0)), axis=1), fold)
        tall = tall.reshape(count * 2, 8, 128)
        on_c = iota((count * 2, 8, 128), 1) == (iota((count * 2, 8, 128), 2) >> 4)
        tall = jnp.where(on_c, tall, 0.0).reshape(count, 2, 8, 128)
        return [jnp.concatenate([tall[i, 0], tall[i, 1]], axis=1) for i in range(count)]

    def summed(codes, rows):
        factors = []
        for i in range(len(codes)):
            factors += split(jnp.concatenate(rows[i * 8 : i * 8 + 8], axis=0))
        return dot(
            jnp.concatenate([selection(code) for code in codes], axis=1),
            jnp.concatenate(factors, axis=0),
        )

    def wide(value):
        return jnp.concatenate(split(value), axis=1)

    own = tuple(range(8))
    z_odd = (z_at & 1) == 1
    none = jnp.zeros((8, 256), F32)
    parts, codes = [], []
    for x in range(2):
        y = [yv[k, x] for k in range(FACES)]
        at = [[y[k][e * 16 : e * 16 + 16] for e in range(8)] for k in (5, 6)]
        lhs = (
            [y[0], yv[1 + x, 1 - x], y[4][:64], y[3][64:]]
            + [at[1 - (e & 1)][e] for e in own]
            + [at[e & 1][e] for e in (1, 2, 5, 6)]
        )
        partners = (
            own + own + tuple(e ^ 4 for e in own) + tuple(e ^ 1 for e in own) + (2, 1, 6, 5)
        )
        parts += picked(dot(wide(jnp.concatenate(lhs, axis=0)), own_rhs[x]), partners)
        other = 1 - x
        codes += [
            owner[x] * 8.0 + slots[x][0],
            owner[other] * 8.0 + slots[other][2 - other],
            owner[x] * 8.0 + jnp.where(y_high, slots[x][3], slots[x][4]),
            owner[x] * 8.0 + jnp.where(z_odd, slots[x][5], slots[x][6]),
            owner[x] * 8.0
            + jnp.where(z_at == 1, slots[x][6], jnp.where(z_at == 2, slots[x][5], -1000.0)),
        ]
    inner_rows = jnp.zeros((64, 256), F32)
    for x in range(2):
        part = flat(parts[x * 36 : x * 36 + 36])
        padded = part[:32] + [none, part[32], part[33], none, none, part[34], part[35], none]
        inner_rows += summed(codes[x * 5 : x * 5 + 5], padded)

    def put(at, rows):
        for o in range(AGGS):
            for h in range(rows.shape[1] // 128):
                msg[pl.ds(o * 48 + at + h * 8, 8), :] = rows[
                    o * 8 : o * 8 + 8, h * 128 : (h + 1) * 128
                ]

    def rows_of(device_at, at, count):
        return pl.ds(pl.multiple_of(device_at * 48 + at, 16), count)

    def send(d, at, count):
        target = device(0, 0, d)
        pltpu.make_async_remote_copy(
            src_ref=msg.at[rows_of(target[2], at, count)],
            dst_ref=recv.at[rows_of(gz, at, count)],
            send_sem=row_send.at[0], recv_sem=row_recv.at[0],
            device_id=target, device_id_type=MESH,
        ).start()

    later = {d: late(1 if d > 0 else -1, abs(d)) for d in (2, -2, 3, -3)}
    later[4] = jnp.where(gz < nz // 2, late(1, 4), late(-1, 4))

    def send_all(at, count):
        for d in (1, -1):
            send(d, at, count)
        for d in later:
            pl.when(~later[d])(functools.partial(send, d, at, count))

    put(0, inner_rows)
    learn(2, False)
    send_all(0, 16)

    def when(flag, value, other):
        return jnp.where(jnp.full((1, 128), flag), value, other)

    label = [
        [
            when(inside[0], slots[0][1] + 1.0, 0.0),
            when(inside[1], slots[1][2] + 9.0, 0.0),
        ],
        [
            jnp.where(
                y_high,
                when(inside[3], slots[x][4] + 9.0, 0.0),
                when(inside[2], slots[x][3] + 1.0, 0.0),
            )
            for x in range(2)
        ],
        [
            jnp.where(
                z_at == 0,
                when(inside[4], slots[x][5] + 1.0, 0.0),
                jnp.where(z_at == 3, when(inside[5], slots[x][6] + 9.0, 0.0), 0.0),
            )
            for x in range(2)
        ],
    ]
    row, lane_all = iota((128, 128), 0), iota((128, 128), 1)
    once = ((lane_all & 7) == 0) & (lane_all < 64)
    which, who = [], []
    for x in range(2):
        value = jnp.where(
            row < 4, label[0][x], jnp.where(row < 8, label[1][x], jnp.where(row < 12, label[2][x], 0.0))
        )
        value = jnp.where(once & ((row & 3).astype(F32) == place[x]), value, 0.0)
        which.append(value.astype(BF16))
        who.append((iota((8, 128), 0).astype(F32) == owner[x]).astype(BF16))
    labels = lax.dot_general(
        jnp.concatenate(who, axis=1), jnp.concatenate(which, axis=1),
        (((1,), (1,)), ((), ())), preferred_element_type=F32,
    )

    edge_codes = [
        code[0],
        code[1],
        jnp.where(y_high, pltpu.roll(code[1], 32, 1), code[0]) + 4.0,
        jnp.where(y_high, code[1], pltpu.roll(code[0], 96, 1)) + 4.0,
    ]
    edge_codes = [when(inside[i], edge_codes[i], -1.0) for i in range(4)]
    z_code = jnp.full((1, 128), -1.0, F32)
    for side in range(2):
        for x in range(2):
            for y in range(2):
                to, at = side * 4 + x * 2 + y, y * 4 + side * 3
                turn = (8 * (to - at)) % 128
                value = pltpu.roll(code[x], turn, 1) if turn else code[x]
                z_code = jnp.where(element == to, when(inside[4 + side], value, -1.0), z_code)

    for face in range(6):
        pl.when(inside[face])(functools.partial(halo_wait, face))

    def halo_rhs(face):
        return stacked(sides_in[face] if face < 4 else columns_of(slabs[2]))

    def rows_y(k, y):
        return jnp.concatenate([yv[k, x, y * 64 : y * 64 + 64] for x in range(2)], axis=0)

    def rows_z(k, z):
        return [
            yv[k, x, y * 64 + z * 16 : y * 64 + z * 16 + 16] for x in range(2) for y in range(2)
        ]

    ends = jnp.concatenate(rows_z(5, 0) + rows_z(6, 3), axis=0)
    sides = [yv[1, 0], yv[2, 1], rows_y(3, 0), rows_y(4, 1), ends]
    parts = []
    for i in range(5):
        parts += picked(dot(wide(sides[i]), halo_rhs(i)), own)
    rows = flat(parts)
    put(16, summed(edge_codes, rows[:32]))
    edges = summed([z_code], rows[32:])
    put(32, edges[:, :128] + pltpu.roll(edges[:, 128:], 4, 0))
    for o in range(AGGS):
        msg[pl.ds(o * 48 + 40, 1), :] = labels[o : o + 1]

    send_all(16, 25)
    stay = pltpu.make_async_copy(
        msg.at[rows_of(gz, 0, 41)], recv.at[rows_of(gz, 0, 41)], local_sem.at[0]
    )
    stay.start()
    for stage in range(3):
        learn(stage, True)
        for d in (stage + 2, -stage - 2) if stage < 2 else (4,):
            pl.when(later[d])(functools.partial(send, d, 0, 41))

    others = pltpu.make_async_remote_copy(
        src_ref=msg.at[pl.ds(0, 287)], dst_ref=recv.at[pl.ds(0, 287)],
        send_sem=row_send.at[0], recv_sem=row_recv.at[0],
        device_id=device(0, 0, 1), device_id_type=MESH,
    )
    others.wait_send()
    others.wait_recv()
    stay.wait()


def spread(recv, out_hbm, out_ref, sem):
    pieces = []

    def write(start, lanes):
        piece = (slice(None), pl.ds(start, lanes))
        pieces.append(
            pltpu.make_async_copy(out_ref.at[piece], out_hbm.at[piece], sem.at[len(pieces)])
        )
        pieces[-1].start()

    def came(row):
        return recv[pl.ds(row, 8, stride=48), :]

    for s in range(AGGS):
        for h in range(2):
            out_ref[:, s * 256 + h * 128 : s * 256 + h * 128 + 128] = came(h * 8 + s)
    write(0, AGGS * 256)
    marks = came(40)
    for axis in range(3):
        first, step = (16 + axis * 4, 8) if axis < 2 else (32, 4)
        values = [[came(first + h * step + p) for h in range(2)] for p in range(4)]
        tags = [
            jnp.broadcast_to(marks[:, axis * 4 + p : axis * 4 + p + 1], (8, 128)) for p in range(4)
        ]
        for column in range(16):
            hits = [tag == column + 1.0 for tag in tags]
            for h in range(2):
                total = jnp.where(hits[0], values[0][h], 0.0)
                for p in range(1, 4):
                    total += jnp.where(hits[p], values[p][h], 0.0)
                at_lane = (AGGS * (1 + 2 * axis) + column) * 256 + h * 128
                out_ref[:, at_lane : at_lane + 128] = total
        write(AGGS * (1 + 2 * axis) * 256, AGGS * 512)
    for piece in pieces:
        piece.wait()


def solution(mesh):
    sizes = (mesh.shape["gx"], mesh.shape["gy"], mesh.shape["gz"])

    def shards(fine_blocks, prolong, agg_map, owner_map):
        fine = fine_blocks.transpose(0, 1, 3, 2, 4).reshape(2, 2, 7, 4, 32, 128)
        fine = fine.transpose(0, 1, 2, 4, 3, 5).reshape(3584, 128)
        base = prolong.reshape(2, 2, 4, 8, 128).transpose(0, 1, 3, 2, 4)
        fine, base, agg_map, owner_map = (
            pltpu.with_memory_space_constraint(value, pltpu.HBM)
            for value in (fine, base, agg_map, owner_map)
        )
        rows = pl.pallas_call(
            functools.partial(kernel, sizes),
            out_shape=jax.ShapeDtypeStruct((384, 128), F32),
            in_specs=[pl.BlockSpec(memory_space=pltpu.HBM)] * 4,
            out_specs=pl.BlockSpec(memory_space=pltpu.VMEM),
            scratch_shapes=[
                pltpu.VMEM((3584, 128), F32),
                pltpu.VMEM((3, 8, 8, 128), F32),
                pltpu.VMEM((4, 64, 128), F32),
                pltpu.VMEM((4, 64, 128), F32),
                pltpu.VMEM((4,) + agg_map.shape[1:], jnp.int32),
                pltpu.VMEM((1, 1, AGGS), jnp.int32),
                pltpu.VMEM((FACES, 2, 128, 128), F32),
                pltpu.VMEM((384, 128), F32),
                pltpu.SemaphoreType.DMA((4,)),
                pltpu.SemaphoreType.DMA((6,)),
                pltpu.SemaphoreType.DMA((6,)),
                pltpu.SemaphoreType.DMA((1,)),
                pltpu.SemaphoreType.DMA((1,)),
                pltpu.SemaphoreType.REGULAR((2, 3)),
            ],
            compiler_params=pltpu.CompilerParams(
                collective_id=0, has_side_effects=True, vmem_limit_bytes=16 << 20
            ),
        )(fine, base, agg_map, owner_map)
        result = pl.pallas_call(
            spread,
            out_shape=jax.ShapeDtypeStruct((AGGS, 7 * AGGS * 256), F32),
            in_specs=[pl.BlockSpec(memory_space=pltpu.VMEM)],
            out_specs=pl.BlockSpec(memory_space=pltpu.HBM),
            scratch_shapes=[
                pltpu.VMEM((AGGS, 7 * AGGS * 256), F32),
                pltpu.SemaphoreType.DMA((4,)),
            ],
            compiler_params=pltpu.CompilerParams(vmem_limit_bytes=8 << 20),
        )(rows)
        return result.reshape(1, 1, AGGS, 7 * AGGS * 256)

    placed = (P("gx", "gy", "gz", None, None), P("gx", "gy", "gz", None), P(), P("gx", "gy", "gz"))
    return jax.shard_map(
        shards, mesh=mesh, in_specs=placed, out_specs=P("gx", "gy", "gz", None), check_vma=False
    )
```
